32 devices in a mesh: grad: 16 (over z, y, core), flow: 2 (over x).
Axes of the slice: x: 2, y: 2, z: 4, core: 2. Of those that a mesh axis runs over, the one named last changes fastest.
Arguments:
- bead_pos: float32 [3, 16, 8192], P(None, 'grad', 'flow'), may hold values from 0 to 11, as said below
- bead_vel: float32 [3, 16, 8192], P(None, 'grad', 'flow'), may hold values from -5 to 5
- noise_angle: float32 [2, 16, 8192], P(None, 'grad', 'flow'), may hold values from -3.140625 to 3.140625
- occupancy: int32 [16, 128], P('grad', 'flow'), may hold values from 32 to 64
- image_shift: int32 [1], replicated, may hold values from 0 to 127
- strain: float32 [1], replicated, may hold values from 0.38 to 0.48
Outputs:
- new_pos: float32 [3, 16, 8192], P(None, 'grad', 'flow')
- new_vel: float32 [3, 16, 8192], P(None, 'grad', 'flow')
- stress_profile: float32 [16], P('grad')
The draws below stay inside these ranges and needn't reach their ends.
Inputs may be any that keep to these rules, and one draw needn't show every extreme that they name: `bead_pos`: the first coordinate lies in [0, 2), the second in [0, 1), the third in [0, 64 / 6).
All inputs are finite; a program needn't handle non-finite values.
Results may differ from the reference program's by a relative error of at most 0.0003.
Values sent between devices are 32-bit elements; how exact they have to be, the bound alone decides.
No kernel may reach another device: no remote copies, remote signals or barrier semaphores. Data moves between devices by JAX's collectives and lax.ppermute only.
A program may use at most 64 MiB of HBM per device.

```python
import math
import jax
import jax.numpy as jnp
from jax import lax

TB = 64
NX = 128
NY = 16
SLOTS = 8192


def draw_bead_pos(key, part):
    unit = jax.random.uniform(key, (3, NY, NX * TB), jnp.float32)
    scales = jnp.array([2.0, 1.0, TB / 6.0], jnp.float32)[:, None, None]
    return unit * scales


def touch_ends(result, own_key, low, largest):
    longest = result.shape.index(max(result.shape))
    spots = []
    for shift in (0, 1):
        where = [jax.random.randint(jax.random.fold_in(own_key, axis), (), 0, length) for axis, length in enumerate(result.shape)]
        where[longest] = (where[longest] + shift) % result.shape[longest]
        spots.append(tuple(where))
    return result.at[spots[0]].set(low).at[spots[1]].set(largest)


def block_levels(key, dims, split, low, top_value):
    level = 1.0
    for axis_at, shards_of in split:
        draws = jax.random.uniform(jax.random.fold_in(jax.random.fold_in(key, 6), axis_at), (shards_of,), jnp.float32, low / len(split), top_value / len(split))
        level = level * jnp.repeat(jnp.exp(draws), dims[axis_at] // shards_of).reshape((-1,) + (1,) * (len(dims) - 1 - axis_at))
    return level


def scatter_about(key, dims, scale, most, cuts=(), kind=jnp.bfloat16):
    drawn = scale * jax.random.normal(key, dims, jnp.float32)
    if cuts:
        drawn = drawn * block_levels(key, dims, cuts, -0.22, 0.18)
    return jnp.clip(drawn, -most, most).astype(kind)


def setup_inputs(seed: int = 0) -> dict:
    key_of = jax.random.split(jax.random.key(seed), 7)
    bead_pos = draw_bead_pos(jax.random.fold_in(key_of[6], 71), 0)
    bead_vel = scatter_about(key_of[1], (3, NY, SLOTS), 1.0, 5.0, ((1, 16), (2, 2)), jnp.float32)
    noise_angle = jnp.clip(jax.random.uniform(key_of[2], (2, NY, SLOTS), jnp.float32, -3.140625, 3.140625), -3.140625, 3.140625)
    occupancy = touch_ends(jax.random.randint(key_of[3], (NY, NX), TB // 2, TB + 1), jax.random.fold_in(key_of[3], 1), TB // 2, TB).astype(jnp.int32)
    image_shift = jax.random.randint(key_of[4], (1,), 0, NX).astype(jnp.int32)
    strain = jnp.clip(jax.random.uniform(key_of[5], (1,), jnp.float32, 0.38, 0.48), 0.38, 0.48)
    return {"bead_pos": bead_pos, "bead_vel": bead_vel, "noise_angle": noise_angle, "occupancy": occupancy, "image_shift": image_shift, "strain": strain}


repulsion = 25.0
friction = 4.5
noise_gain = 15.0
time_step = 0.04
shear_rate = 0.25
root_two = 1.4142135623730951


def live_slots(occupancy):
    rows_here = occupancy.shape[0]
    width = occupancy.shape[1] * TB
    slot_index = lax.broadcasted_iota(jnp.int32, (rows_here, width), 1) % TB
    limits = jnp.repeat(occupancy, TB, axis=1)
    return (slot_index < limits).astype(jnp.float32)


def band_forces(slab_band, strain_now):
    all_tiles = slab_band.shape[2] // TB
    centre_tiles = all_tiles - 2
    block_tiles = math.gcd(32, centre_tiles)
    tile_grid = slab_band.reshape(slab_band.shape[0], 3, all_tiles, TB)
    box_depth = TB / 6.0
    slot_row = lax.broadcasted_iota(jnp.int32, (TB, 3 * TB), 0)
    slot_col = lax.broadcasted_iota(jnp.int32, (TB, 3 * TB), 1)
    itself = (slot_col == slot_row + TB).astype(jnp.float32)
    offset = jnp.repeat(jnp.array([2.0, 0.0, -2.0], jnp.float32), TB)

    def one_block(first_tile):
        centre = lax.dynamic_slice_in_dim(tile_grid[:, 1], first_tile + 1, block_tiles, 1)[:, :, :, None]
        forces = jnp.zeros((3, block_tiles, TB), jnp.float32)
        virial = jnp.zeros((), jnp.float32)
        for band_row in range(3):
            nearby = lax.dynamic_slice_in_dim(tile_grid[:, band_row], first_tile, block_tiles + 2, 1)
            partners = jnp.concatenate([nearby[:, column:column + block_tiles] for column in range(3)], 2)[:, :, None, :]
            sep_x = centre[0] - partners[0] + offset
            sep_y = centre[1] - partners[1] + (1.0 - band_row)
            sep_z = centre[2] - partners[2]
            sep_z = jnp.where(sep_z > 0.5 * box_depth, sep_z - box_depth, sep_z)
            sep_z = jnp.where(sep_z < -0.5 * box_depth, sep_z + box_depth, sep_z)
            phys_x = sep_x + strain_now * sep_y
            paired = centre[7] * partners[7]
            if band_row == 1:
                paired = paired * (1.0 - itself)
            weight = jnp.maximum(1.0 - phys_x * phys_x - sep_y * sep_y - sep_z * sep_z, 0.0) * paired
            approach = phys_x * (centre[3] - partners[3]) + sep_y * (centre[4] - partners[4]) + sep_z * (centre[5] - partners[5])
            random_kick = root_two * jnp.cos(centre[6] - partners[6])
            magnitude = weight * (repulsion + noise_gain * random_kick - friction * weight * approach)
            forces = forces + jnp.stack([jnp.sum(magnitude * phys_x, -1), jnp.sum(magnitude * sep_y, -1), jnp.sum(magnitude * sep_z, -1)])
            virial = virial + 0.5 * jnp.sum(magnitude * phys_x * sep_y)
        return forces, virial

    starts = jnp.arange(0, centre_tiles, block_tiles, dtype=jnp.int32)
    block_forces, block_virials = lax.map(one_block, starts)
    forces = jnp.transpose(block_forces, (1, 0, 2, 3)).reshape(3, centre_tiles * TB)
    return forces, jnp.sum(block_virials)


def advance(positions, velocity, forces, strain_now):
    vel_x = velocity[0] + time_step * (forces[0] - shear_rate * velocity[1])
    vel_y = velocity[1] + time_step * forces[1]
    vel_z = velocity[2] + time_step * forces[2]
    pos_x = positions[0] + time_step * (vel_x - strain_now * vel_y)
    pos_y = positions[1] + time_step * vel_y
    pos_z = positions[2] + time_step * vel_z
    return jnp.stack([pos_x, pos_y, pos_z]), jnp.stack([vel_x, vel_y, vel_z]), strain_now + shear_rate * time_step


def reference(bead_pos, bead_vel, noise_angle, occupancy, image_shift, strain):
    live_mask = live_slots(occupancy)
    image_tiles = image_shift[0]
    strain_now = strain[0]
    positions, velocity = bead_pos, bead_vel
    running = jnp.zeros((NY,), jnp.float32)
    for step_index in range(2):
        fields = jnp.concatenate([positions, velocity, noise_angle[step_index][None], live_mask[None]], 0)
        below_row = jnp.roll(fields[:, NY - 1], -image_tiles * TB, axis=1)
        above_row = jnp.roll(fields[:, 0], image_tiles * TB, axis=1)
        extended = jnp.concatenate([below_row[:, None], fields, above_row[:, None]], 1)
        extended = jnp.concatenate([extended[:, :, -TB:], extended, extended[:, :, :TB]], 2)

        def one_row(row_index):
            return band_forces(lax.dynamic_slice_in_dim(extended, row_index, 3, 1), strain_now)

        row_forces, virials = lax.map(one_row, jnp.arange(NY, dtype=jnp.int32))
        forces = jnp.transpose(row_forces, (1, 0, 2))
        kinetic = jnp.sum(live_mask * velocity[0] * velocity[1], axis=1)
        running = running + kinetic + virials
        positions, velocity, strain_now = advance(positions, velocity, forces, strain_now)
    row_numbers = jnp.arange(NY, dtype=jnp.int32)
    parity = (row_numbers % 2).astype(jnp.float32)
    shifted_x = positions[0] + parity[:, None] + positions[1]
    stacked = jnp.concatenate([shifted_x[None], positions[1:], velocity], 0)
    remapped = jax.vmap(lambda segment, device_hops: jnp.roll(segment, device_hops * TB, axis=1), in_axes=(1, 0), out_axes=1)(stacked, row_numbers // 2)
    box_depth = TB / 6.0
    stress_profile = (-running / (2.0 * NX * 2.0 * box_depth)).astype(jnp.float32)
    return remapped[:3], remapped[3:], stress_profile
```

```python
import functools
import math

import jax
import jax.numpy as jnp
from jax import lax
from jax.experimental import pallas as pl
from jax.experimental.pallas import tpu as pltpu
from jax.sharding import PartitionSpec as P

TB = 64
HALF = TB // 2

repulsion = 25.0
friction = 4.5
noise_gain = 15.0
time_step = 0.04
shear_rate = 0.25
root_two = 1.4142135623730951

DEPTH = TB / 6.0
UNIT = 1.0 / DEPTH
SPEED = friction * DEPTH**3
KICK = math.sqrt(noise_gain * root_two)
FAR = 1.0e6

FIELDS = 8


def lanes_of(shape):
    return lax.broadcasted_iota(jnp.int32, shape, 1)


def live_beads(occ_ref, occ_tmp, tiles):
    occ_tmp[...] = jnp.zeros_like(occ_tmp)
    occ_tmp[0:1, 0:tiles] = occ_ref[...]
    row = jnp.broadcast_to(occ_tmp[0:1, :], (8, 2 * tiles))
    row = jnp.where(lanes_of(row.shape) < tiles, row, pltpu.roll(row, tiles, 1))
    limit = jnp.broadcast_to(row[0:1, :], (HALF, 2 * tiles))
    upper = (lanes_of(limit.shape) >= tiles).astype(jnp.int32)
    slot = lax.broadcasted_iota(jnp.int32, limit.shape, 0) + HALF * upper
    return (slot < limit).astype(jnp.float32)


def write_sent(state, kick, live, strain, sent_ref, edge_ref, turn):
    pos_x, pos_y, pos_z, vel_x, vel_y, vel_z = state
    sent_ref[0] = (pos_x + strain * pos_y) * UNIT
    sent_ref[1] = jnp.where(live > 0.0, pos_y * UNIT, FAR)
    sent_ref[2] = pos_z * UNIT
    sent_ref[3] = vel_x * SPEED
    sent_ref[4] = vel_y * SPEED
    sent_ref[5] = vel_z * SPEED
    sent_ref[6] = kick[0]
    sent_ref[7] = kick[1]
    tiles = sent_ref.shape[2] // 2
    for group in range(2):
        for k in range(4):
            turn[k * HALF : (k + 1) * HALF, :] = sent_ref[4 * group + k]
        turned = turn[...].T
        for side, tile in enumerate((0, tiles - 1)):
            for half in range(2):
                at = group * 4 + side * 2 + half
                row = half * tiles + tile
                edge_ref[at : at + 1, :] = turned[row : row + 1, :]


def prepare_kernel(strain_ref, pos_ref, vel_ref, noise_ref, occ_ref, state_ref, later_ref, live_ref, sent_ref, edge_ref, turn, occ_tmp):
    tiles = occ_ref.shape[1]
    live = live_beads(occ_ref, occ_tmp, tiles)
    live_ref[...] = live
    rows = pos_ref.shape[1]
    low = lanes_of((rows, 2 * TB)) < TB
    sources = [pos_ref.at[0], pos_ref.at[1], pos_ref.at[2], vel_ref.at[0], vel_ref.at[1], vel_ref.at[2], noise_ref.at[0], noise_ref.at[1]]
    fields = []
    first = lanes_of((HALF, 2 * tiles)) < tiles
    for pair in range(4):
        one = sources[2 * pair][...]
        two = sources[2 * pair + 1][...]
        even = jnp.where(low, one, pltpu.roll(two, TB, 1))
        odd = jnp.where(low, pltpu.roll(one, TB, 1), two)
        for copy in range(2):
            turn[pl.ds(copy * tiles, rows, stride=2), :] = even
            turn[pl.ds(copy * tiles + 1, rows, stride=2), :] = odd
        turned = turn[...].T
        for k in range(2):
            whole = turned[k * TB : (k + 1) * TB]
            fields.append(jnp.where(first, whole[:HALF], whole[HALF:]))
    for k in range(6):
        state_ref[k] = fields[k]
    later_ref[0] = KICK * jnp.cos(fields[7])
    later_ref[1] = KICK * jnp.sin(fields[7])
    kick = (KICK * jnp.cos(fields[6]), KICK * jnp.sin(fields[6]))
    write_sent(fields[:6], kick, live, strain_ref[0], sent_ref, edge_ref, turn)


def edge_columns(edge_ref, side):
    turned = edge_ref[...].T
    columns = []
    for field in range(FIELDS):
        group, k = divmod(field, 4)
        rows = turned[k * HALF : (k + 1) * HALF]
        at = group * 4 + side * 2
        columns.append((rows[:, at : at + 1], rows[:, at + 1 : at + 2]))
    return columns


def place_partners(partners, base, own_row, next_row, last_row, left_edge, right_edge, offset, image, shift_x, shift_y, tiles):
    shape = (HALF, 2 * tiles)
    lane = lanes_of(shape)
    first = lane < tiles
    left = edge_columns(left_edge, 1)
    right = edge_columns(right_edge, 0)
    for field in range(FIELDS):
        here = own_row(field)
        for half in range(2):
            if half == 0:
                inner = here
            else:
                inner = pltpu.roll(here, tiles, 1)
            outer = jnp.where(lane == tiles, right[field][half], left[field][half])
            if next_row is not None:
                beyond = next_row(field)
                if half == 0:
                    beyond = pltpu.roll(beyond, tiles, 1)
                if last_row is not None:
                    final = last_row(field)
                    if half == 0:
                        final = pltpu.roll(final, tiles, 1)
                    at_end = jnp.logical_and(lane == 2 * tiles - 1, offset == 0)
                    beyond = jnp.where(at_end, final, beyond)
                outer = jnp.where(image > 0, beyond, outer)
            window = jnp.where(first, inner, outer)
            if next_row is not None:
                window = pltpu.roll(window, offset, 1)
            for column in range(3):
                toward = column - 1
                low = window if toward == 0 else pltpu.roll(window, -toward % (2 * tiles), 1)
                high = pltpu.roll(window, tiles - toward, 1)
                placed = jnp.where(first, low, high)
                if field == 0:
                    placed = placed + (2.0 * toward * UNIT + shift_x)
                if field == 1:
                    placed = placed + shift_y
                at = base + column * TB + half * HALF
                partners[field, at : at + HALF, :] = placed


def own_fields(state_ref, sent_ref, field):
    return state_ref[1] * UNIT if field == 1 else sent_ref[field]


def pair_sums(state_ref, sent_ref, partners, count, one_shift, unroll):
    lanes = sent_ref.shape[2]
    kappa = UNIT * UNIT
    pieces = HALF // 8
    together = 2
    out = []
    for start in range(0, pieces, together):
        mine = []
        for piece in range(start, start + together):
            rows = slice(piece * 8, piece * 8 + 8)
            values = [sent_ref[field, rows, :] for field in range(FIELDS)]
            values[1] = state_ref[1, rows, :] * UNIT
            mine.append(values)

        def body(step, sums):
            sums = [list(entry) for entry in sums]
            for inner in range(unroll):
                at = step * unroll + inner
                theirs = [partners[field, pl.ds(at, 8, stride=0), :] for field in range(FIELDS)]
                for k in range(together):
                    me = mine[k]
                    dx = me[0] - theirs[0]
                    dy = me[1] - theirs[1]
                    dz = me[2] - theirs[2]
                    fold = jnp.round(dz)
                    if one_shift:
                        fold = jnp.clip(fold, -1.0, 1.0)
                    dz = dz - fold
                    weight = jnp.maximum((kappa - dx * dx) - (dy * dy + dz * dz), 0.0)
                    approach = dx * (me[3] - theirs[3]) + dy * (me[4] - theirs[4]) + dz * (me[5] - theirs[5])
                    kick = (me[6] * theirs[6] + me[7] * theirs[7]) + repulsion
                    size = weight * (kick - weight * approach)
                    push = size * dx
                    sums[k][0] = sums[k][0] + push
                    sums[k][1] = sums[k][1] + size * dy
                    sums[k][2] = sums[k][2] + size * dz
                    sums[k][3] = sums[k][3] + push * dy
            return tuple(tuple(entry) for entry in sums)

        zero = jnp.zeros((8, lanes), jnp.float32)
        init = tuple((zero,) * 4 for _ in range(together))
        out.extend(lax.fori_loop(0, count // unroll, body, init))
    return out


def row_kernel(state_ref, sent_ref, live_ref, left_edge, right_edge, force_ref, sum_ref, partners):
    tiles = sent_ref.shape[2] // 2
    place_partners(partners, 0, lambda field: sent_ref[field], None, None, left_edge, right_edge, None, None, 0.0, 0.0, tiles)
    sums = pair_sums(state_ref, sent_ref, partners, 3 * TB, True, 4)
    total = jnp.zeros(sum_ref.shape, jnp.float32)
    for piece, (fx, fy, fz, vir) in enumerate(sums):
        rows = slice(piece * 8, piece * 8 + 8)
        for k, value in enumerate((fx, fy, fz)):
            force_ref[k, rows, :] = value
        kinetic = state_ref[3, rows, :] * state_ref[4, rows, :]
        total = total + live_ref[rows, :] * (0.5 * DEPTH**4 * vir + kinetic)
    sum_ref[...] = total


def cross_kernel(last, flows, ints_ref, strain_ref, *refs):
    refs = list(refs)
    state_ref, sent_ref, live_ref, later_ref, force_ref, sum_ref = refs[:6]
    below, above = refs[6:8]
    image_rows = refs[8 : 8 + flows - 1]
    edges = refs[8 + flows - 1 : 12 + flows - 1]
    rest = refs[12 + flows - 1 :]
    strain = strain_ref[0]
    tiles = sent_ref.shape[2] // 2
    partners, turn = rest[-2], rest[-1]
    for index, straight in enumerate((below, above)):
        toward = 2 * index - 1
        image = ints_ref[4 * index]
        block = ints_ref[4 * index + 1]
        offset = ints_ref[4 * index + 2]
        choices = [straight] + image_rows

        def pick(field, ahead):
            value = choices[0][field]
            for k in range(1, flows):
                value = jnp.where((block + ahead) % flows == k, choices[k][field], value)
            return value

        place_partners(
            partners,
            index * 3 * TB,
            lambda field: pick(field, 0),
            lambda field: pick(field, 1),
            None if flows == 2 else lambda field: pick(field, flows - 1),
            edges[2 * index],
            edges[2 * index + 1],
            offset,
            image,
            toward * strain * UNIT,
            toward * UNIT,
            tiles,
        )
    sums = pair_sums(state_ref, sent_ref, partners, 6 * TB, True, 4)
    total = sum_ref[...]
    forces = [[], [], []]
    for piece, entry in enumerate(sums):
        rows = slice(piece * 8, piece * 8 + 8)
        total = total + live_ref[rows, :] * (0.5 * DEPTH**4 * entry[3])
        for k in range(3):
            forces[k].append((entry[k] + force_ref[k, rows, :]) * (live_ref[rows, :] * DEPTH**3))
    force = [jnp.concatenate(parts, 0) for parts in forces]
    state = [state_ref[k] for k in range(6)]
    vel_x = state[3] + time_step * (force[0] - shear_rate * state[4])
    vel_y = state[4] + time_step * force[1]
    vel_z = state[5] + time_step * force[2]
    pos_x = state[0] + time_step * (vel_x - strain * vel_y)
    pos_y = state[1] + time_step * vel_y
    pos_z = state[2] + time_step * vel_z
    state = [pos_x, pos_y, pos_z, vel_x, vel_y, vel_z]
    if not last:
        new_state, new_sent, new_edge, new_sum = rest[:4]
        for k in range(6):
            new_state[k] = state[k]
        new_sum[...] = total
        later = strain + shear_rate * time_step
        write_sent(state, (later_ref[0], later_ref[1]), live_ref[...], later, new_sent, new_edge, turn)
        return
    flat_ref, new_sum = rest[:2]
    parity = ints_ref[8].astype(jnp.float32)
    state[0] = pos_x + parity + pos_y
    new_sum[...] = total
    rows = tiles // 2
    lane = lanes_of((rows, 2 * TB))
    for group in range(2):
        for k in range(4):
            if 4 * group + k < 6:
                turn[k * HALF : (k + 1) * HALF, :] = state[4 * group + k]
        turn[...] = turn[...].T
        for k in range(4):
            if 4 * group + k >= 6:
                continue
            value = None
            for odd in range(2):
                for half in range(2):
                    piece = turn[pl.ds(half * tiles + odd, rows, stride=2), :]
                    target = odd * TB + half * HALF
                    piece = pltpu.roll(piece, (target - k * HALF) % (2 * TB), 1)
                    value = piece if value is None else jnp.where(lane >= target, piece, value)
            flat_ref[4 * group + k] = value


def finish_kernel(scale, tail_rows, ints_ref, flat_ref, tail_ref, sum_ref, other_ref, pos_ref, vel_ref, stress_ref, line):
    rows = flat_ref.shape[1]
    skip = ints_ref[9]
    lane = lanes_of((rows, 2 * TB))
    row0 = skip // 2
    odd = skip % 2
    for k in range(6):
        line[0:tail_rows, :] = tail_ref[k]
        line[tail_rows : tail_rows + rows, :] = flat_ref[k]
        one = line[pl.ds(row0, rows), :]
        two = line[pl.ds(row0 + odd, rows), :]
        swapped = jnp.where(lane < TB, pltpu.roll(one, TB, 1), pltpu.roll(two, TB, 1))
        value = jnp.where(odd > 0, swapped, one)
        if k < 3:
            pos_ref[k] = value
        else:
            vel_ref[k - 3] = value
    total = sum_ref[...] + other_ref[...]
    total = jnp.sum(jnp.sum(total, axis=0, keepdims=True), axis=1, keepdims=True)
    stress_ref[...] = jnp.broadcast_to(total * scale, stress_ref.shape)


def vmem(count):
    return [pl.BlockSpec(memory_space=pltpu.VMEM)] * count


def smem(count):
    return [pl.BlockSpec(memory_space=pltpu.SMEM)] * count


def f32(*shape):
    return jax.ShapeDtypeStruct(shape, jnp.float32)


def per_device(bead_pos, bead_vel, noise_angle, occupancy, image_shift, strain):
    grads = lax.axis_size("grad")
    flows = lax.axis_size("flow")
    grad = lax.axis_index("grad")
    flow = lax.axis_index("flow")
    tiles = occupancy.shape[1]
    lanes = 2 * tiles
    rows = tiles * TB // (2 * TB)
    axes = ("grad", "flow")

    def device(g, f):
        return (g % grads) * flows + f % flows

    def moved(x, up, along):
        pairs = [(device(g, f), device(g + up, f + along)) for g in range(grads) for f in range(flows)]
        return lax.ppermute(x, axes, pairs)

    def across(x, k):
        pairs = [(device(-1, f + k), device(0, f)) for f in range(flows)]
        pairs += [(device(0, f + k), device(-1, f)) for f in range(flows)]
        return lax.ppermute(x, axes, pairs)

    bottom = (grad == 0).astype(jnp.int32)
    top = (grad == grads - 1).astype(jnp.int32)
    ahead = bottom * (image_shift[0] % (tiles * flows))
    behind = top * ((tiles * flows - image_shift[0] % (tiles * flows)) % (tiles * flows))
    tail_tiles = grads // 2
    tail_rows = (tail_tiles + 1) // 2
    skip = 2 * tail_rows - grad // 2
    ints = jnp.stack(
        [
            bottom, ahead // tiles, (lanes - ahead % tiles) % lanes, bottom,
            top, behind // tiles, (lanes - behind % tiles) % lanes, top,
            grad % 2, skip,
        ]
    ).astype(jnp.int32)

    turn = pltpu.VMEM((lanes, 2 * TB), jnp.float32)
    prepare = pl.pallas_call(
        prepare_kernel,
        out_shape=(
            f32(6, HALF, lanes), f32(2, HALF, lanes), f32(HALF, lanes),
            f32(FIELDS, HALF, lanes), f32(8, 2 * TB),
        ),
        in_specs=smem(1) + vmem(4),
        out_specs=vmem(5),
        scratch_shapes=[turn, pltpu.VMEM((8, lanes), jnp.int32)],
        name="prepare",
    )
    state, later, live, sent, edge = prepare(
        strain,
        bead_pos.reshape(3, rows, 2 * TB),
        bead_vel.reshape(3, rows, 2 * TB),
        noise_angle.reshape(2, rows, 2 * TB),
        occupancy,
    )

    def exchange(sent, edge):
        if flows == 2:
            side = moved(edge, 0, 1)
            sides = (side, side)
            low = moved(edge, 1, 1)
            high = moved(edge, -1, 1)
            corners = (low, low, high, high)
        else:
            sides = (moved(edge, 0, 1), moved(edge, 0, -1))
            corners = (moved(edge, 1, 1), moved(edge, 1, -1), moved(edge, -1, 1), moved(edge, -1, -1))
        below = moved(sent, 1, 0)
        above = moved(sent, -1, 0)
        images = [across(sent, k) for k in range(1, flows)]
        return sides, corners, below, above, images

    pair_flops = 35 * TB * TB * tiles
    sums = None
    strain_now = strain
    for step in range(2):
        last = step == 1
        sides, corners, below, above, images = exchange(sent, edge)
        force, part = pl.pallas_call(
            row_kernel,
            out_shape=(f32(3, HALF, lanes), f32(8, lanes)),
            in_specs=vmem(5),
            out_specs=vmem(2),
            scratch_shapes=[pltpu.VMEM((FIELDS, 3 * TB, lanes), jnp.float32)],
            cost_estimate=pl.CostEstimate(flops=3 * pair_flops, bytes_accessed=1 << 19, transcendentals=0),
            name=f"row_pairs_{step}",
        )(state, sent, live, sides[0], sides[1])
        if sums is not None:
            part = part + sums
        outs = (
            (f32(6, rows, 2 * TB), f32(8, lanes))
            if last
            else (f32(6, HALF, lanes), f32(FIELDS, HALF, lanes), f32(8, 2 * TB), f32(8, lanes))
        )
        results = pl.pallas_call(
            functools.partial(cross_kernel, last, flows),
            out_shape=outs,
            in_specs=smem(2) + vmem(12 + flows - 1),
            out_specs=vmem(len(outs)),
            scratch_shapes=[pltpu.VMEM((FIELDS, 6 * TB, lanes), jnp.float32), turn],
            cost_estimate=pl.CostEstimate(flops=6 * pair_flops, bytes_accessed=1 << 20, transcendentals=0),
            name=f"cross_pairs_{step}",
        )(ints, strain_now, state, sent, live, later, force, part, below, above, *images, *corners)
        if last:
            flat, sums = results
        else:
            state, sent, edge, sums = results
            strain_now = strain_now + shear_rate * time_step

    tail = lax.slice_in_dim(flat, rows - tail_rows, rows, axis=1)
    tail = lax.ppermute(tail, "flow", [(f, (f + 1) % flows) for f in range(flows)])
    if flows & (flows - 1):
        raise NotImplementedError
    hop = 1
    other = lax.ppermute(sums, "flow", [(f, f ^ hop) for f in range(flows)])
    while 2 * hop < flows:
        hop *= 2
        sums = sums + other
        other = lax.ppermute(sums, "flow", [(f, f ^ hop) for f in range(flows)])
    scale = -1.0 / (2.0 * tiles * flows * 2.0 * DEPTH)
    new_pos, new_vel, stress = pl.pallas_call(
        functools.partial(finish_kernel, scale, tail_rows),
        out_shape=(f32(3, rows, 2 * TB), f32(3, rows, 2 * TB), f32(1, 128)),
        in_specs=smem(1) + vmem(4),
        out_specs=vmem(3),
        scratch_shapes=[pltpu.VMEM((tail_rows + rows + 8, 2 * TB), jnp.float32)],
        name="finish",
    )(ints, flat, tail, sums, other)
    return (
        new_pos.reshape(bead_pos.shape),
        new_vel.reshape(bead_vel.shape),
        stress[0, :1],
    )


def solution(mesh):
    in_specs = (
        P(None, "grad", "flow"),
        P(None, "grad", "flow"),
        P(None, "grad", "flow"),
        P("grad", "flow"),
        P(),
        P(),
    )
    out_specs = (P(None, "grad", "flow"), P(None, "grad", "flow"), P("grad"))
    return jax.shard_map(
        per_device, mesh=mesh, in_specs=in_specs, out_specs=out_specs, check_vma=False
    )
```

```python
import functools
import math

import jax
import jax.numpy as jnp
from jax import lax
from jax.experimental import pallas as pl
from jax.experimental.pallas import tpu as pltpu
from jax.sharding import PartitionSpec as P

TB = 64
HALF = TB // 2

repulsion = 25.0
friction = 4.5
noise_gain = 15.0
time_step = 0.04
shear_rate = 0.25
root_two = 1.4142135623730951

DEPTH = TB / 6.0
UNIT = 1.0 / DEPTH
SPEED = friction * DEPTH**3
KICK = math.sqrt(noise_gain * root_two)
FAR = 1.0e6

FIELDS = 8
TOGETHER = 1
UNROLL = 8
STRIDE = 2


def lanes_of(shape):
    return lax.broadcasted_iota(jnp.int32, shape, 1)


def live_beads(occ_ref, occ_tmp, tiles):
    occ_tmp[...] = jnp.zeros_like(occ_tmp)
    occ_tmp[0:1, 0:tiles] = occ_ref[...]
    row = jnp.broadcast_to(occ_tmp[0:1, :], (8, 2 * tiles))
    row = jnp.where(lanes_of(row.shape) < tiles, row, pltpu.roll(row, tiles, 1))
    limit = jnp.broadcast_to(row[0:1, :], (HALF, 2 * tiles))
    upper = (lanes_of(limit.shape) >= tiles).astype(jnp.int32)
    slot = lax.broadcasted_iota(jnp.int32, limit.shape, 0) + HALF * upper
    return (slot < limit).astype(jnp.float32)


def part(ref, field):
    return ref[field * HALF : (field + 1) * HALF, :]


def write_sent(state, kick, live, strain, sent_ref, turn):
    pos_x, pos_y, pos_z, vel_x, vel_y, vel_z = state
    fields = [
        (pos_x + strain * pos_y) * UNIT,
        jnp.where(live > 0.0, pos_y * UNIT, FAR),
        pos_z * UNIT,
        vel_x * SPEED,
        vel_y * SPEED,
        vel_z * SPEED,
        kick[0],
        kick[1],
    ]
    tiles = sent_ref.shape[1] // 2
    for field in range(FIELDS):
        sent_ref[field * HALF : (field + 1) * HALF, :] = fields[field]
    for group in range(2):
        for k in range(4):
            turn[k * HALF : (k + 1) * HALF, :] = fields[4 * group + k]
        turned = turn[...].T
        for side, tile in enumerate((0, tiles - 1)):
            for half in range(2):
                at = FIELDS * HALF + group * 4 + side * 2 + half
                row = half * tiles + tile
                sent_ref[at : at + 1, :] = turned[row : row + 1, :]


def prepare_kernel(strain_ref, pos_ref, vel_ref, noise_ref, occ_ref, state_ref, later_ref, live_ref, sent_ref, turn, occ_tmp):
    tiles = occ_ref.shape[1]
    live = live_beads(occ_ref, occ_tmp, tiles)
    live_ref[...] = live
    rows = pos_ref.shape[1]
    low = lanes_of((rows, 2 * TB)) < TB
    sources = [pos_ref.at[0], pos_ref.at[1], pos_ref.at[2], vel_ref.at[0], vel_ref.at[1], vel_ref.at[2], noise_ref.at[0], noise_ref.at[1]]
    fields = []
    first = lanes_of((HALF, 2 * tiles)) < tiles
    for pair in range(4):
        one = sources[2 * pair][...]
        two = sources[2 * pair + 1][...]
        even = jnp.where(low, one, pltpu.roll(two, TB, 1))
        odd = jnp.where(low, pltpu.roll(one, TB, 1), two)
        for copy in range(2):
            turn[pl.ds(copy * tiles, rows, stride=2), :] = even
            turn[pl.ds(copy * tiles + 1, rows, stride=2), :] = odd
        turned = turn[...].T
        for k in range(2):
            whole = turned[k * TB : (k + 1) * TB]
            fields.append(jnp.where(first, whole[:HALF], whole[HALF:]))
    for k in range(6):
        state_ref[k] = fields[k]
    later_ref[0] = KICK * jnp.cos(fields[7])
    later_ref[1] = KICK * jnp.sin(fields[7])
    kick = (KICK * jnp.cos(fields[6]), KICK * jnp.sin(fields[6]))
    write_sent(fields[:6], kick, live, strain_ref[0], sent_ref, turn)


def place_partners(partners, own_row, outside, offset, shift_x, shift_y, tiles):
    shape = (HALF, 2 * tiles)
    first = lanes_of(shape) < tiles
    widest = jnp.zeros(shape, jnp.float32)
    for field in range(FIELDS):
        here = own_row(field)
        for half in range(2):
            inner = here if half == 0 else pltpu.roll(here, tiles, 1)
            window = jnp.where(first, inner, outside(field, half))
            if offset is not None:
                window = pltpu.roll(window, offset, 1)
            for column in range(3):
                toward = column - 1
                low = window if toward == 0 else pltpu.roll(window, -toward % (2 * tiles), 1)
                high = pltpu.roll(window, tiles - toward, 1)
                placed = jnp.where(first, low, high)
                if field == 0:
                    placed = placed + (2.0 * toward * UNIT + shift_x)
                if field == 1:
                    placed = placed + shift_y
                if field == 2:
                    widest = jnp.maximum(widest, jnp.abs(placed - 0.5))
                at = column * TB + half * HALF
                partners[field, at : at + HALF, :] = placed
    return widest


def interact(me, theirs, one_shift):
    dx = me[0] - theirs[0]
    dy = me[1] - theirs[1]
    dz = me[2] - theirs[2]
    fold = jnp.round(dz)
    if one_shift:
        fold = jnp.clip(fold, -1.0, 1.0)
    dz = dz - fold
    weight = jnp.maximum((UNIT * UNIT - dx * dx) - (dy * dy + dz * dz), 0.0)
    approach = dx * (me[3] - theirs[3]) + dy * (me[4] - theirs[4]) + dz * (me[5] - theirs[5])
    kick = (me[6] * theirs[6] + me[7] * theirs[7]) + repulsion
    size = weight * (kick - weight * approach)
    return size * dx, size * dy, size * dz, dy


def keep_own(own, state_ref, sent_ref, live_ref):
    for field in range(FIELDS):
        own[field] = part(sent_ref, field)
    own[1] = jnp.where(live_ref[...] > 0.0, state_ref[1] * UNIT, -FAR)


def strayed(row_ref):
    return jnp.abs(part(row_ref, 2) - 0.5)


def guarded(widest, run):
    if widest is None:
        run(False)
        return
    near = jnp.max(widest) < 0.74
    pl.when(near)(lambda: run(False))
    pl.when(jnp.logical_not(near))(lambda: run(True))


def one_sided(own, partners, count, one_shift, sums_ref):
    for piece in range(HALF // 8):
        rows = slice(piece * 8, piece * 8 + 8)
        me = [own[field, rows, :] for field in range(FIELDS)]

        def body(step, sums):
            for inner in range(UNROLL):
                at = step * UNROLL + inner
                theirs = [partners[field, pl.ds(at, 8, stride=0), :] for field in range(FIELDS)]
                fx, fy, fz, dy = interact(me, theirs, one_shift)
                sums = (sums[0] + fx, sums[1] + fy, sums[2] + fz, sums[3] + fx * dy)
            return sums

        zero = jnp.zeros((8, own.shape[2]), jnp.float32)
        sums = lax.fori_loop(0, count // UNROLL, body, (zero,) * 4)
        for k in range(4):
            sums_ref[k, rows, :] = sums[k]


def both_sided(own, cyclic, low, count, one_shift, force_ref, backs):
    pieces = HALF // 8
    stride = max(1, len(backs))

    def body(step, sums):
        sums = list(sums)
        for inner in range(stride):
            start = low + step * stride + inner
            for piece in range(pieces):
                at = start + piece * 8
                me = [own[field, piece * 8 : piece * 8 + 8, :] for field in range(FIELDS)]
                theirs = [cyclic[field, pl.ds(at, 8), :] for field in range(FIELDS)]
                push = interact(me, theirs, one_shift)
                for k in range(3):
                    sums[piece * 3 + k] = sums[piece * 3 + k] + push[k]
                    if backs:
                        back = backs[inner]
                        back[k, pl.ds(at, 8), :] = back[k, pl.ds(at, 8), :] + push[k]
        return tuple(sums)

    spots = [(k, slice(piece * 8, piece * 8 + 8)) for piece in range(pieces) for k in range(3)]
    init = tuple(force_ref[k, rows, :] for k, rows in spots)
    sums = lax.fori_loop(0, count // stride, body, init)
    for (k, rows), value in zip(spots, sums):
        force_ref[k, rows, :] = value


def fill_cyclic(cyclic, row_ref, column, shift_x, shift_y):
    lanes = row_ref.shape[1]
    tiles = lanes // 2
    for field in range(FIELDS):
        value = part(row_ref, field)
        if column:
            value = pltpu.roll(value, lanes - 1, 1)
        if field == 0:
            value = value + (2.0 * column * UNIT + shift_x)
        if field == 1:
            value = value + shift_y
            if column:
                value = jnp.where(lanes_of(value.shape) % tiles == tiles - 1, FAR, value)
        cyclic[field, 0:HALF, :] = value
        cyclic[field, HALF : 2 * HALF, :] = pltpu.roll(value, tiles, 1)
        cyclic[field, 2 * HALF : 3 * HALF, :] = value


def clear(backs):
    for back in backs:
        back[...] = jnp.zeros_like(back)


def fold_back(backs, k, column):
    total = backs[0][k]
    for back in backs[1:]:
        total = total + back[k]
    folded = total[:HALF] + total[2 * HALF :] + pltpu.roll(total[HALF : 2 * HALF], total.shape[1] // 2, 1)
    return pltpu.roll(folded, 1, 1) if column else folded


def edge_rows(own_edge, mate_edge, side):
    lane = lanes_of(own_edge.shape)
    width = own_edge.shape[1]
    rows = []
    for field in range(FIELDS):
        group, k = divmod(field, 4)
        value = None
        for place, (edge, half) in enumerate(((own_edge, 0), (own_edge, 1), (mate_edge, 0), (mate_edge, 1))):
            at = group * 4 + side * 2 + half
            turned = pltpu.roll(edge, (place - k) * HALF % width, 1)
            row = jnp.broadcast_to(turned[at : at + 1, :], edge.shape)
            value = row if value is None else jnp.where(lane >= place * HALF, row, value)
        rows.append(value)
    return rows


def edge_pairs(own, left_ref, right_ref, side, strain, one_shift, found):
    lanes = own.shape[2]
    tiles = lanes // 2
    lane = lanes_of((8, lanes))
    for tile, ref, at, column in ((0, left_ref, 1, -1.0), (tiles - 1, right_ref, 0, 1.0)):
        theirs = edge_rows(ref[0:8, :], ref[8:16, :], at)
        of_mate = (lanes_of(theirs[0].shape) >= 2 * HALF).astype(jnp.float32)
        theirs[0] = theirs[0] + (2.0 * column * UNIT + side * strain * UNIT * of_mate)
        theirs[1] = theirs[1] + side * UNIT * of_mate
        for half in range(2):
            spot = half * tiles + tile
            for piece in range(HALF // 8):
                rows = slice(piece * 8, piece * 8 + 8)
                me = [
                    jnp.broadcast_to(own[field, rows, :][:, spot : spot + 1], (8, lanes))
                    for field in range(FIELDS)
                ]
                fx, fy, fz, dy = interact(me, theirs, one_shift)
                for k, value in enumerate((fx, fy, fz, fx * dy)):
                    total = jnp.sum(value, axis=1, keepdims=True)
                    found[k, rows, :] = found[k, rows, :] + jnp.where(lane == spot, total, 0.0)


def side_of(other):
    even = 1 - lax.axis_index("grad") % 2
    return (1 - 2 * even if other else 2 * even - 1).astype(jnp.float32)


def row_kernel(step, state_ref, sent_ref, live_ref, force_ref, sum_ref, own, same, follow, *backs):
    keep_own(own, state_ref, sent_ref, live_ref)
    fill_cyclic(same, sent_ref, 0, 0.0, 0.0)
    fill_cyclic(follow, sent_ref, 1, 0.0, 0.0)
    clear(backs)
    force_ref[...] = jnp.zeros_like(force_ref)
    here, beyond = backs[:STRIDE], backs[STRIDE:]

    def run(one_shift):
        both_sided(own, same, 0, HALF, one_shift, force_ref, here)
        both_sided(own, same, HALF, 1, one_shift, force_ref, ())
        both_sided(own, follow, 0, TB, one_shift, force_ref, beyond)

    guarded(strayed(sent_ref) if step else None, run)
    for k in range(3):
        force_ref[k] = force_ref[k] - (fold_back(here, k, 0) + fold_back(beyond, k, 1))
    total = jnp.zeros(sum_ref.shape, jnp.float32)
    for piece in range(HALF // 8):
        rows = slice(piece * 8, piece * 8 + 8)
        kinetic = state_ref[3, rows, :] * state_ref[4, rows, :]
        virial = DEPTH**3 * force_ref[0, rows, :] * state_ref[1, rows, :]
        total = total + live_ref[rows, :] * (kinetic + virial)
    sum_ref[...] = total


def mate_kernel(step, strain_ref, state_ref, sent_ref, live_ref, mate_ref, force_ref, given_ref, edge_ref, own, same, follow, *backs):
    strain = strain_ref[0] + step * shear_rate * time_step
    side = side_of(False)
    keep_own(own, state_ref, sent_ref, live_ref)
    fill_cyclic(same, mate_ref, 0, side * strain * UNIT, side * UNIT)
    fill_cyclic(follow, mate_ref, 1, side * strain * UNIT, side * UNIT)
    clear(backs)
    force_ref[...] = jnp.zeros_like(force_ref)
    here, beyond = backs[:STRIDE], backs[STRIDE:]
    low = lax.axis_index("grad") % 2

    def run(one_shift):
        both_sided(own, same, low, HALF, one_shift, force_ref, here)
        both_sided(own, follow, 0, TB, one_shift, force_ref, beyond)

    guarded(jnp.maximum(strayed(sent_ref), strayed(mate_ref)) if step else None, run)
    given = [fold_back(here, k, 0) + fold_back(beyond, k, 1) for k in range(3)]
    for k in range(3):
        given_ref[k * HALF : (k + 1) * HALF, :] = given[k]
    virial = own[1] * force_ref[0] - (part(mate_ref, 1) + side * UNIT) * given[0]
    given_ref[3 * HALF : 3 * HALF + 8, :] = sum(virial[at : at + 8] for at in range(0, HALF, 8))
    edge_ref[0:8, :] = sent_ref[FIELDS * HALF : FIELDS * HALF + 8, :]
    edge_ref[8:16, :] = mate_ref[FIELDS * HALF : FIELDS * HALF + 8, :]


def other_kernel(step, flows, grads, strain_ref, shift_ref, *refs):
    refs = list(refs)
    state_ref, sent_ref, live_ref, later_ref, row_force, row_sum, mate_force, given, taken, left, right, old_sum = refs[:12]
    blocks = refs[12 : 12 + flows]
    rest = refs[12 + flows :]
    last = step == 1
    strain = strain_ref[0] + step * shear_rate * time_step
    tiles = sent_ref.shape[1] // 2
    lanes = 2 * tiles
    partners, turn, found, own = rest[-4:]
    grad = lax.axis_index("grad")
    side = side_of(True)
    whole = tiles * flows
    shift = lax.rem(shift_ref[0], whole)
    start = jnp.where(grad == 0, shift, jnp.where(grad == grads - 1, lax.rem(whole - shift, whole), 0))
    block = start // tiles
    offset = lax.rem(lanes - lax.rem(start, tiles), lanes)

    def pick(field, ahead):
        value = part(blocks[0], field)
        for k in range(1, flows):
            value = jnp.where(lax.rem(block + ahead, flows) == k, part(blocks[k], field), value)
        return value

    def outside(field, half):
        beyond = pick(field, 1)
        if flows > 2:
            lane = lanes_of(beyond.shape)
            final = jnp.logical_and(lane % tiles == tiles - 1, offset == 0)
            beyond = jnp.where(final, pick(field, flows - 1), beyond)
        return pltpu.roll(beyond, tiles, 1) if half == 0 else beyond

    widest = place_partners(
        partners, lambda field: pick(field, 0), outside, offset, side * strain * UNIT, side * UNIT, tiles
    )
    keep_own(own, state_ref, sent_ref, live_ref)
    widest = jnp.maximum(widest, strayed(sent_ref))
    for ref in (left, right):
        lane = lanes_of(ref.shape)
        row = lax.broadcasted_iota(jnp.int32, ref.shape, 0)
        is_z = jnp.logical_and(row % 8 < 4, lane // HALF == 2)
        reach = jnp.where(is_z, jnp.abs(ref[...] - 0.5), 0.0)
        widest = jnp.maximum(widest, jnp.concatenate([reach, reach], 0))

    def run(one_shift):
        one_sided(own, partners, 3 * TB, one_shift, found)
        edge_pairs(own, left, right, side_of(False), strain, one_shift, found)

    guarded(widest if step else None, run)
    total = row_sum[...] + (0.5 * DEPTH**4) * (given[3 * HALF : 3 * HALF + 8, :] + taken[3 * HALF : 3 * HALF + 8, :])
    if last:
        total = total + old_sum[...]
    force = []
    for k in range(3):
        value = found[k] + (row_force[k] + (mate_force[k] - part(taken, k)))
        force.append(value * (live_ref[...] * DEPTH**3))
    for piece in range(HALF // 8):
        rows = slice(piece * 8, piece * 8 + 8)
        total = total + live_ref[rows, :] * (0.5 * DEPTH**4 * found[3, rows, :])
    state = [state_ref[k] for k in range(6)]
    vel_x = state[3] + time_step * (force[0] - shear_rate * state[4])
    vel_y = state[4] + time_step * force[1]
    vel_z = state[5] + time_step * force[2]
    pos_x = state[0] + time_step * (vel_x - strain * vel_y)
    pos_y = state[1] + time_step * vel_y
    pos_z = state[2] + time_step * vel_z
    state = [pos_x, pos_y, pos_z, vel_x, vel_y, vel_z]
    if not last:
        new_state, new_sent, new_sum = rest[:3]
        for k in range(6):
            new_state[k] = state[k]
        new_sum[...] = total
        later = strain + shear_rate * time_step
        write_sent(state, (later_ref[0], later_ref[1]), live_ref[...], later, new_sent, turn)
        return
    flat_ref, tail_ref, new_sum = rest[:3]
    tail_rows = (grads // 2 + 1) // 2
    parity = lax.rem(grad, 2).astype(jnp.float32)
    state[0] = pos_x + parity + pos_y
    new_sum[...] = total
    rows = tiles // 2
    lane = lanes_of((rows, 2 * TB))
    for group in range(2):
        for k in range(4):
            if 4 * group + k < 6:
                turn[k * HALF : (k + 1) * HALF, :] = state[4 * group + k]
        turn[...] = turn[...].T
        for k in range(4):
            if 4 * group + k >= 6:
                continue
            value = None
            for odd in range(2):
                for half in range(2):
                    piece = turn[pl.ds(half * tiles + odd, rows, stride=2), :]
                    target = odd * TB + half * HALF
                    piece = pltpu.roll(piece, (target - k * HALF) % (2 * TB), 1)
                    value = piece if value is None else jnp.where(lane >= target, piece, value)
            flat_ref[4 * group + k] = value
            at = (4 * group + k) * tail_rows
            tail_ref[at : at + tail_rows, :] = value[rows - tail_rows :, :]
    tail_ref[6 * tail_rows : 6 * tail_rows + 8, :] = total


def finish_kernel(scale, tail_rows, flat_ref, tail_ref, sum_ref, other_ref, pos_ref, vel_ref, stress_ref, line):
    rows = flat_ref.shape[1]
    skip = 2 * tail_rows - lax.axis_index("grad") // 2
    lane = lanes_of((rows, 2 * TB))
    row0 = skip // 2
    odd = skip % 2
    for k in range(6):
        line[0:tail_rows, :] = tail_ref[k * tail_rows : (k + 1) * tail_rows, :]
        line[tail_rows : tail_rows + rows, :] = flat_ref[k]
        one = line[pl.ds(row0, rows), :]
        two = line[pl.ds(row0 + odd, rows), :]
        swapped = jnp.where(lane < TB, pltpu.roll(one, TB, 1), pltpu.roll(two, TB, 1))
        value = jnp.where(odd > 0, swapped, one)
        if k < 3:
            pos_ref[k] = value
        else:
            vel_ref[k - 3] = value
    at = 6 * tail_rows if other_ref.shape == tail_ref.shape else 0
    total = sum_ref[...] + other_ref[at : at + 8, :]
    total = jnp.sum(jnp.sum(total, axis=0, keepdims=True), axis=1, keepdims=True)
    stress_ref[...] = jnp.broadcast_to(total * scale, stress_ref.shape)


def vmem(count):
    return [pl.BlockSpec(memory_space=pltpu.VMEM)] * count


def smem(count):
    return [pl.BlockSpec(memory_space=pltpu.SMEM)] * count


def f32(*shape):
    return jax.ShapeDtypeStruct(shape, jnp.float32)


def per_device(bead_pos, bead_vel, noise_angle, occupancy, image_shift, strain):
    grads = lax.axis_size("grad")
    flows = lax.axis_size("flow")
    tiles = occupancy.shape[1]
    lanes = 2 * tiles
    rows = tiles * TB // (2 * TB)

    def from_mate(x):
        return lax.ppermute(x, "grad", [(g, g ^ 1) for g in range(grads)])

    def from_flow(x, ahead):
        return lax.ppermute(x, "flow", [((f + ahead) % flows, f) for f in range(flows)])

    tail_rows = (grads // 2 + 1) // 2

    turn = pltpu.VMEM((lanes, 2 * TB), jnp.float32)
    prepare = pl.pallas_call(
        prepare_kernel,
        out_shape=(
            f32(6, HALF, lanes), f32(2, HALF, lanes), f32(HALF, lanes),
            f32(FIELDS * HALF + 8, lanes),
        ),
        in_specs=smem(1) + vmem(4),
        out_specs=vmem(4),
        scratch_shapes=[turn, pltpu.VMEM((8, lanes), jnp.int32)],
        name="prepare",
    )
    state, later, live, sent = prepare(
        strain,
        bead_pos.reshape(3, rows, 2 * TB),
        bead_vel.reshape(3, rows, 2 * TB),
        noise_angle.reshape(2, rows, 2 * TB),
        occupancy,
    )

    pair_flops = 35 * 3 * TB * TB * tiles
    cost = pl.CostEstimate(flops=pair_flops, bytes_accessed=1 << 19, transcendentals=0)
    partners = pltpu.VMEM((FIELDS, 3 * TB, lanes), jnp.float32)
    own = pltpu.VMEM((FIELDS, HALF, lanes), jnp.float32)
    cyclic = [pltpu.VMEM((FIELDS, 3 * HALF, lanes), jnp.float32)] * 2
    backs = [pltpu.VMEM((3, 3 * HALF, lanes), jnp.float32)] * (2 * STRIDE)
    sums = jnp.zeros((8, lanes), jnp.float32)
    for step in range(2):
        last = step == 1
        mate = from_mate(sent)
        other = lax.ppermute(sent, "grad", [(g, (g + 2 * (g % 2) - 1) % grads) for g in range(grads)])
        mate_force, given, edges = pl.pallas_call(
            functools.partial(mate_kernel, step),
            out_shape=(f32(3, HALF, lanes), f32(3 * HALF + 8, lanes), f32(16, lanes)),
            in_specs=smem(1) + vmem(4),
            out_specs=vmem(3),
            scratch_shapes=[own, *cyclic, *backs],
            cost_estimate=cost,
            name=f"mate_pairs_{step}",
        )(strain, state, sent, live, mate)
        other, given = lax.optimization_barrier((other, given))
        taken = from_mate(given)
        left = from_flow(edges, -1)
        right = left if flows == 2 else from_flow(edges, 1)
        blocks = [other] + [from_flow(other, k) for k in range(1, flows)]
        row_force, row_sum = pl.pallas_call(
            functools.partial(row_kernel, step),
            out_shape=(f32(3, HALF, lanes), f32(8, lanes)),
            in_specs=vmem(3),
            out_specs=vmem(2),
            scratch_shapes=[own, *cyclic, *backs],
            cost_estimate=cost,
            name=f"row_pairs_{step}",
        )(state, sent, live)
        outs = (
            (f32(6, rows, 2 * TB), f32(6 * tail_rows + 8, 2 * TB), f32(8, lanes))
            if last
            else (f32(6, HALF, lanes), f32(FIELDS * HALF + 8, lanes), f32(8, lanes))
        )
        results = pl.pallas_call(
            functools.partial(other_kernel, step, flows, grads),
            out_shape=outs,
            in_specs=smem(2) + vmem(12 + flows),
            out_specs=vmem(len(outs)),
            scratch_shapes=[partners, turn, pltpu.VMEM((4, HALF, lanes), jnp.float32), own],
            cost_estimate=cost,
            name=f"other_pairs_{step}",
        )(strain, image_shift, state, sent, live, later, row_force, row_sum, mate_force, given, taken, left, right, sums, *blocks)
        if last:
            flat, tail, sums = results
        else:
            state, sent, sums = results

    tail = lax.ppermute(tail, "flow", [(f, (f + 1) % flows) for f in range(flows)])
    if flows & (flows - 1):
        raise NotImplementedError
    partial = tail
    if flows > 2:
        hop = 1
        partial = lax.ppermute(sums, "flow", [(f, f ^ hop) for f in range(flows)])
        while 2 * hop < flows:
            hop *= 2
            sums = sums + partial
            partial = lax.ppermute(sums, "flow", [(f, f ^ hop) for f in range(flows)])
    scale = -1.0 / (2.0 * tiles * flows * 2.0 * DEPTH)
    new_pos, new_vel, stress = pl.pallas_call(
        functools.partial(finish_kernel, scale, tail_rows),
        out_shape=(f32(3, rows, 2 * TB), f32(3, rows, 2 * TB), f32(1, 128)),
        in_specs=vmem(4),
        out_specs=vmem(3),
        scratch_shapes=[pltpu.VMEM((tail_rows + rows + 8, 2 * TB), jnp.float32)],
        name="finish",
    )(flat, tail, sums, partial)
    return (
        new_pos.reshape(bead_pos.shape),
        new_vel.reshape(bead_vel.shape),
        stress[0, :1],
    )


def solution(mesh):
    in_specs = (
        P(None, "grad", "flow"),
        P(None, "grad", "flow"),
        P(None, "grad", "flow"),
        P("grad", "flow"),
        P(),
        P(),
    )
    out_specs = (P(None, "grad", "flow"), P(None, "grad", "flow"), P("grad"))
    return jax.shard_map(
        per_device, mesh=mesh, in_specs=in_specs, out_specs=out_specs, check_vma=False
    )
```

```python
import functools
import math

import jax
import jax.numpy as jnp
from jax import lax
from jax.experimental import pallas as pl
from jax.experimental.pallas import tpu as pltpu
from jax.sharding import PartitionSpec as P

TB = 64
HALF = TB // 2

repulsion = 25.0
friction = 4.5
noise_gain = 15.0
time_step = 0.04
shear_rate = 0.25
root_two = 1.4142135623730951

DEPTH = TB / 6.0
UNIT = 1.0 / DEPTH
SPEED = friction * DEPTH**3
KICK = math.sqrt(noise_gain * root_two)
FAR = 1.0e6

FIELDS = 8
TOGETHER = 1
UNROLL = 16
STRIDE = 4
BACKS = 2


def lanes_of(shape):
    return lax.broadcasted_iota(jnp.int32, shape, 1)


def live_beads(occ_ref, occ_tmp, tiles):
    occ_tmp[...] = jnp.zeros_like(occ_tmp)
    occ_tmp[0:1, 0:tiles] = occ_ref[...]
    row = jnp.broadcast_to(occ_tmp[0:1, :], (8, 2 * tiles))
    row = jnp.where(lanes_of(row.shape) < tiles, row, pltpu.roll(row, tiles, 1))
    limit = jnp.broadcast_to(row[0:1, :], (HALF, 2 * tiles))
    upper = (lanes_of(limit.shape) >= tiles).astype(jnp.int32)
    slot = lax.broadcasted_iota(jnp.int32, limit.shape, 0) + HALF * upper
    return (slot < limit).astype(jnp.float32)


def part(ref, field):
    return ref[field * HALF : (field + 1) * HALF, :]


def write_sent(state, kick, live, strain, sent_ref, turn):
    pos_x, pos_y, pos_z, vel_x, vel_y, vel_z = state
    fields = [
        (pos_x + strain * pos_y) * UNIT,
        jnp.where(live > 0.0, pos_y * UNIT, FAR),
        pos_z * UNIT,
        vel_x * SPEED,
        vel_y * SPEED,
        vel_z * SPEED,
        kick[0],
        kick[1],
    ]
    tiles = sent_ref.shape[1] // 2
    for field in range(FIELDS):
        sent_ref[field * HALF : (field + 1) * HALF, :] = fields[field]
    for group in range(2):
        for k in range(4):
            turn[k * HALF : (k + 1) * HALF, :] = fields[4 * group + k]
        turned = turn[...].T
        for side, tile in enumerate((0, tiles - 1)):
            for half in range(2):
                at = FIELDS * HALF + group * 4 + side * 2 + half
                row = half * tiles + tile
                sent_ref[at : at + 1, :] = turned[row : row + 1, :]


def prepare_kernel(strain_ref, pos_ref, vel_ref, noise_ref, occ_ref, state_ref, later_ref, live_ref, sent_ref, turn, occ_tmp):
    tiles = occ_ref.shape[1]
    live = live_beads(occ_ref, occ_tmp, tiles)
    live_ref[...] = live
    rows = pos_ref.shape[1]
    low = lanes_of((rows, 2 * TB)) < TB
    sources = [pos_ref.at[0], pos_ref.at[1], pos_ref.at[2], vel_ref.at[0], vel_ref.at[1], vel_ref.at[2], noise_ref.at[0], noise_ref.at[1]]
    fields = []
    first = lanes_of((HALF, 2 * tiles)) < tiles
    for pair in range(4):
        one = sources[2 * pair][...]
        two = sources[2 * pair + 1][...]
        even = jnp.where(low, one, pltpu.roll(two, TB, 1))
        odd = jnp.where(low, pltpu.roll(one, TB, 1), two)
        for copy in range(2):
            turn[pl.ds(copy * tiles, rows, stride=2), :] = even
            turn[pl.ds(copy * tiles + 1, rows, stride=2), :] = odd
        turned = turn[...].T
        for k in range(2):
            whole = turned[k * TB : (k + 1) * TB]
            fields.append(jnp.where(first, whole[:HALF], whole[HALF:]))
    for k in range(6):
        state_ref[k] = fields[k]
    later_ref[0] = KICK * jnp.cos(fields[7])
    later_ref[1] = KICK * jnp.sin(fields[7])
    kick = (KICK * jnp.cos(fields[6]), KICK * jnp.sin(fields[6]))
    write_sent(fields[:6], kick, live, strain_ref[0], sent_ref, turn)


def place_partners(partners, own_row, outside, offset, shift_x, shift_y, tiles):
    shape = (HALF, 2 * tiles)
    first = lanes_of(shape) < tiles
    widest = jnp.zeros(shape, jnp.float32)
    for field in range(FIELDS):
        here = own_row(field)
        for half in range(2):
            inner = here if half == 0 else pltpu.roll(here, tiles, 1)
            window = jnp.where(first, inner, outside(field, half))
            if offset is not None:
                window = pltpu.roll(window, offset, 1)
            for column in range(3):
                toward = column - 1
                low = window if toward == 0 else pltpu.roll(window, -toward % (2 * tiles), 1)
                high = pltpu.roll(window, tiles - toward, 1)
                placed = jnp.where(first, low, high)
                if field == 0:
                    placed = placed + (2.0 * toward * UNIT + shift_x)
                if field == 1:
                    placed = placed + shift_y
                if field == 2:
                    widest = jnp.maximum(widest, jnp.abs(placed - 0.5))
                at = column * TB + half * HALF
                partners[field, at : at + HALF, :] = placed
    return widest


def interact(me, theirs, one_shift):
    dx = me[0] - theirs[0]
    dy = me[1] - theirs[1]
    dz = me[2] - theirs[2]
    fold = jnp.round(dz)
    if one_shift:
        fold = jnp.clip(fold, -1.0, 1.0)
    dz = dz - fold
    weight = jnp.maximum((UNIT * UNIT - dx * dx) - (dy * dy + dz * dz), 0.0)
    approach = dx * (me[3] - theirs[3]) + dy * (me[4] - theirs[4]) + dz * (me[5] - theirs[5])
    kick = (me[6] * theirs[6] + me[7] * theirs[7]) + repulsion
    size = weight * (kick - weight * approach)
    return size * dx, size * dy, size * dz, dy


def keep_own(own, state_ref, sent_ref, live_ref):
    for field in range(FIELDS):
        own[field] = part(sent_ref, field)
    own[1] = jnp.where(live_ref[...] > 0.0, state_ref[1] * UNIT, -FAR)


def strayed(row_ref):
    return jnp.abs(part(row_ref, 2) - 0.5)


def guarded(widest, run):
    if widest is None:
        run(False)
        return
    near = jnp.max(widest) < 0.74
    pl.when(near)(lambda: run(False))
    pl.when(jnp.logical_not(near))(lambda: run(True))


def one_sided(own, partners, count, one_shift, sums_ref):
    for piece in range(HALF // 8):
        rows = slice(piece * 8, piece * 8 + 8)
        me = [own[field, rows, :] for field in range(FIELDS)]

        def body(step, sums):
            for inner in range(UNROLL):
                at = step * UNROLL + inner
                theirs = [partners[field, pl.ds(at, 8, stride=0), :] for field in range(FIELDS)]
                fx, fy, fz, dy = interact(me, theirs, one_shift)
                sums = (sums[0] + fx, sums[1] + fy, sums[2] + fz, sums[3] + fx * dy)
            return sums

        zero = jnp.zeros((8, own.shape[2]), jnp.float32)
        sums = lax.fori_loop(0, count // UNROLL, body, (zero,) * 4)
        for k in range(4):
            sums_ref[k, rows, :] = sums[k]


def both_sided(own, cyclic, low, count, one_shift, force_ref, backs):
    pieces = HALF // 8
    stride = STRIDE if backs else 1

    def body(step, sums):
        sums = list(sums)
        for inner in range(stride):
            start = low + step * stride + inner
            for piece in range(pieces):
                at = start + piece * 8
                me = [own[field, piece * 8 : piece * 8 + 8, :] for field in range(FIELDS)]
                theirs = [cyclic[field, pl.ds(at, 8), :] for field in range(FIELDS)]
                push = interact(me, theirs, one_shift)
                for k in range(3):
                    sums[piece * 3 + k] = sums[piece * 3 + k] + push[k]
                    if backs:
                        back = backs[inner % BACKS]
                        back[k, pl.ds(at, 8), :] = back[k, pl.ds(at, 8), :] + push[k]
        return tuple(sums)

    spots = [(k, slice(piece * 8, piece * 8 + 8)) for piece in range(pieces) for k in range(3)]
    init = tuple(force_ref[k, rows, :] for k, rows in spots)
    sums = lax.fori_loop(0, count // stride, body, init)
    for (k, rows), value in zip(spots, sums):
        force_ref[k, rows, :] = value


def fill_cyclic(cyclic, row_ref, column, shift_x, shift_y):
    lanes = row_ref.shape[1]
    tiles = lanes // 2
    for field in range(FIELDS):
        value = part(row_ref, field)
        if column:
            value = pltpu.roll(value, lanes - 1, 1)
        if field == 0:
            value = value + (2.0 * column * UNIT + shift_x)
        if field == 1:
            value = value + shift_y
            if column:
                value = jnp.where(lanes_of(value.shape) % tiles == tiles - 1, FAR, value)
        cyclic[field, 0:HALF, :] = value
        cyclic[field, HALF : 2 * HALF, :] = pltpu.roll(value, tiles, 1)
        cyclic[field, 2 * HALF : 3 * HALF, :] = value


def clear(backs):
    for back in backs:
        back[...] = jnp.zeros_like(back)


def fold_back(backs, k, column):
    total = backs[0][k]
    for back in backs[1:]:
        total = total + back[k]
    folded = total[:HALF] + total[2 * HALF :] + pltpu.roll(total[HALF : 2 * HALF], total.shape[1] // 2, 1)
    return pltpu.roll(folded, 1, 1) if column else folded


def edge_rows(own_edge, mate_edge, side):
    lane = lanes_of(own_edge.shape)
    width = own_edge.shape[1]
    rows = []
    for field in range(FIELDS):
        group, k = divmod(field, 4)
        value = None
        for place, (edge, half) in enumerate(((own_edge, 0), (own_edge, 1), (mate_edge, 0), (mate_edge, 1))):
            at = group * 4 + side * 2 + half
            turned = pltpu.roll(edge, (place - k) * HALF % width, 1)
            row = jnp.broadcast_to(turned[at : at + 1, :], edge.shape)
            value = row if value is None else jnp.where(lane >= place * HALF, row, value)
        rows.append(value)
    return rows


def edge_pairs(own, left_ref, right_ref, side, strain, one_shift, found):
    lanes = own.shape[2]
    tiles = lanes // 2
    lane = lanes_of((8, lanes))
    for tile, ref, at, column in ((0, left_ref, 1, -1.0), (tiles - 1, right_ref, 0, 1.0)):
        theirs = edge_rows(ref[0:8, :], ref[8:16, :], at)
        of_mate = (lanes_of(theirs[0].shape) >= 2 * HALF).astype(jnp.float32)
        theirs[0] = theirs[0] + (2.0 * column * UNIT + side * strain * UNIT * of_mate)
        theirs[1] = theirs[1] + side * UNIT * of_mate
        for half in range(2):
            spot = half * tiles + tile
            for piece in range(HALF // 8):
                rows = slice(piece * 8, piece * 8 + 8)
                me = [
                    jnp.broadcast_to(own[field, rows, :][:, spot : spot + 1], (8, lanes))
                    for field in range(FIELDS)
                ]
                fx, fy, fz, dy = interact(me, theirs, one_shift)
                for k, value in enumerate((fx, fy, fz, fx * dy)):
                    total = jnp.sum(value, axis=1, keepdims=True)
                    found[k, rows, :] = found[k, rows, :] + jnp.where(lane == spot, total, 0.0)


def side_of(other):
    even = 1 - lax.axis_index("grad") % 2
    return (1 - 2 * even if other else 2 * even - 1).astype(jnp.float32)


def row_kernel(step, state_ref, sent_ref, live_ref, force_ref, sum_ref, own, same, follow, *backs):
    keep_own(own, state_ref, sent_ref, live_ref)
    fill_cyclic(same, sent_ref, 0, 0.0, 0.0)
    fill_cyclic(follow, sent_ref, 1, 0.0, 0.0)
    clear(backs)
    force_ref[...] = jnp.zeros_like(force_ref)
    here, beyond = backs[:BACKS], backs[BACKS:]

    def run(one_shift):
        both_sided(own, same, 0, HALF, one_shift, force_ref, here)
        both_sided(own, same, HALF, 1, one_shift, force_ref, ())
        both_sided(own, follow, 0, TB, one_shift, force_ref, beyond)

    guarded(strayed(sent_ref) if step else None, run)
    for k in range(3):
        force_ref[k] = force_ref[k] - (fold_back(here, k, 0) + fold_back(beyond, k, 1))
    total = jnp.zeros(sum_ref.shape, jnp.float32)
    for piece in range(HALF // 8):
        rows = slice(piece * 8, piece * 8 + 8)
        kinetic = state_ref[3, rows, :] * state_ref[4, rows, :]
        virial = DEPTH**3 * force_ref[0, rows, :] * state_ref[1, rows, :]
        total = total + live_ref[rows, :] * (kinetic + virial)
    sum_ref[...] = total


def mate_kernel(step, strain_ref, state_ref, sent_ref, live_ref, mate_ref, force_ref, given_ref, edge_ref, own, same, follow, *backs):
    strain = strain_ref[0] + step * shear_rate * time_step
    side = side_of(False)
    keep_own(own, state_ref, sent_ref, live_ref)
    fill_cyclic(same, mate_ref, 0, side * strain * UNIT, side * UNIT)
    fill_cyclic(follow, mate_ref, 1, side * strain * UNIT, side * UNIT)
    clear(backs)
    force_ref[...] = jnp.zeros_like(force_ref)
    here, beyond = backs[:BACKS], backs[BACKS:]
    low = lax.axis_index("grad") % 2

    def run(one_shift):
        both_sided(own, same, low, HALF, one_shift, force_ref, here)
        both_sided(own, follow, 0, TB, one_shift, force_ref, beyond)

    guarded(jnp.maximum(strayed(sent_ref), strayed(mate_ref)) if step else None, run)
    given = [fold_back(here, k, 0) + fold_back(beyond, k, 1) for k in range(3)]
    for k in range(3):
        given_ref[k * HALF : (k + 1) * HALF, :] = given[k]
    virial = own[1] * force_ref[0] - (part(mate_ref, 1) + side * UNIT) * given[0]
    given_ref[3 * HALF : 3 * HALF + 8, :] = sum(virial[at : at + 8] for at in range(0, HALF, 8))
    edge_ref[0:8, :] = sent_ref[FIELDS * HALF : FIELDS * HALF + 8, :]
    edge_ref[8:16, :] = mate_ref[FIELDS * HALF : FIELDS * HALF + 8, :]


def other_kernel(step, flows, grads, strain_ref, shift_ref, *refs):
    refs = list(refs)
    state_ref, sent_ref, live_ref, later_ref, row_force, row_sum, mate_force, given, taken, left, right = refs[:11]
    blocks = refs[11 : 11 + flows]
    rest = refs[11 + flows :]
    last = step == 1
    if last:
        old_sum, rest = rest[0], rest[1:]
    strain = strain_ref[0] + step * shear_rate * time_step
    tiles = sent_ref.shape[1] // 2
    lanes = 2 * tiles
    partners, turn, found, own = rest[-4:]
    grad = lax.axis_index("grad")
    side = side_of(True)
    whole = tiles * flows
    shift = lax.rem(shift_ref[0], whole)
    start = jnp.where(grad == 0, shift, jnp.where(grad == grads - 1, lax.rem(whole - shift, whole), 0))
    block = start // tiles
    offset = lax.rem(lanes - lax.rem(start, tiles), lanes)

    def pick(field, ahead):
        value = part(blocks[0], field)
        for k in range(1, flows):
            value = jnp.where(lax.rem(block + ahead, flows) == k, part(blocks[k], field), value)
        return value

    def outside(field, half):
        beyond = pick(field, 1)
        if flows > 2:
            lane = lanes_of(beyond.shape)
            final = jnp.logical_and(lane % tiles == tiles - 1, offset == 0)
            beyond = jnp.where(final, pick(field, flows - 1), beyond)
        return pltpu.roll(beyond, tiles, 1) if half == 0 else beyond

    widest = place_partners(
        partners, lambda field: pick(field, 0), outside, offset, side * strain * UNIT, side * UNIT, tiles
    )
    keep_own(own, state_ref, sent_ref, live_ref)
    widest = jnp.maximum(widest, strayed(sent_ref))
    for ref in (left, right):
        lane = lanes_of(ref.shape)
        row = lax.broadcasted_iota(jnp.int32, ref.shape, 0)
        is_z = jnp.logical_and(row % 8 < 4, lane // HALF == 2)
        reach = jnp.where(is_z, jnp.abs(ref[...] - 0.5), 0.0)
        widest = jnp.maximum(widest, jnp.concatenate([reach, reach], 0))

    def run(one_shift):
        one_sided(own, partners, 3 * TB, one_shift, found)
        edge_pairs(own, left, right, side_of(False), strain, one_shift, found)

    guarded(widest if step else None, run)
    total = row_sum[...] + (0.5 * DEPTH**4) * (given[3 * HALF : 3 * HALF + 8, :] + taken[3 * HALF : 3 * HALF + 8, :])
    if last:
        total = total + old_sum[...]
    force = []
    for k in range(3):
        value = found[k] + (row_force[k] + (mate_force[k] - part(taken, k)))
        force.append(value * (live_ref[...] * DEPTH**3))
    for piece in range(HALF // 8):
        rows = slice(piece * 8, piece * 8 + 8)
        total = total + live_ref[rows, :] * (0.5 * DEPTH**4 * found[3, rows, :])
    state = [state_ref[k] for k in range(6)]
    vel_x = state[3] + time_step * (force[0] - shear_rate * state[4])
    vel_y = state[4] + time_step * force[1]
    vel_z = state[5] + time_step * force[2]
    pos_x = state[0] + time_step * (vel_x - strain * vel_y)
    pos_y = state[1] + time_step * vel_y
    pos_z = state[2] + time_step * vel_z
    state = [pos_x, pos_y, pos_z, vel_x, vel_y, vel_z]
    if not last:
        new_state, new_sent, new_sum = rest[:3]
        for k in range(6):
            new_state[k] = state[k]
        new_sum[...] = total
        later = strain + shear_rate * time_step
        write_sent(state, (later_ref[0], later_ref[1]), live_ref[...], later, new_sent, turn)
        return
    flat_ref, tail_ref, new_sum = rest[:3]
    tail_rows = (grads // 2 + 1) // 2
    parity = lax.rem(grad, 2).astype(jnp.float32)
    state[0] = pos_x + parity + pos_y
    new_sum[...] = total
    rows = tiles // 2
    lane = lanes_of((rows, 2 * TB))
    for group in range(2):
        for k in range(4):
            if 4 * group + k < 6:
                turn[k * HALF : (k + 1) * HALF, :] = state[4 * group + k]
        turn[...] = turn[...].T
        for k in range(4):
            if 4 * group + k >= 6:
                continue
            value = None
            for odd in range(2):
                for half in range(2):
                    piece = turn[pl.ds(half * tiles + odd, rows, stride=2), :]
                    target = odd * TB + half * HALF
                    piece = pltpu.roll(piece, (target - k * HALF) % (2 * TB), 1)
                    value = piece if value is None else jnp.where(lane >= target, piece, value)
            flat_ref[4 * group + k] = value
            at = (4 * group + k) * tail_rows
            tail_ref[at : at + tail_rows, :] = value[rows - tail_rows :, :]
    tail_ref[6 * tail_rows : 6 * tail_rows + 8, :] = total


def shift_kernel(tail_rows, flat_ref, pos_ref, vel_ref, line):
    move_tiles(tail_rows, flat_ref, None, pos_ref, vel_ref, line)


def move_tiles(tail_rows, flat_ref, tail_ref, pos_ref, vel_ref, line):
    rows = flat_ref.shape[1]
    skip = 2 * tail_rows - lax.axis_index("grad") // 2
    lane = lanes_of((rows, 2 * TB))
    row0 = skip // 2
    odd = lax.rem(skip, 2)
    for k in range(6):
        if tail_ref is None:
            line[0:tail_rows, :] = jnp.zeros((tail_rows, 2 * TB), jnp.float32)
        else:
            line[0:tail_rows, :] = tail_ref[k * tail_rows : (k + 1) * tail_rows, :]
        line[tail_rows : tail_rows + rows, :] = flat_ref[k]
        one = line[pl.ds(row0, rows), :]
        two = line[pl.ds(row0 + odd, rows), :]
        swapped = jnp.where(lane < TB, pltpu.roll(one, TB, 1), pltpu.roll(two, TB, 1))
        value = jnp.where(odd > 0, swapped, one)
        if k < 3:
            pos_ref[k] = value
        else:
            vel_ref[k - 3] = value


def finish_kernel(scale, tail_rows, flat_ref, tail_ref, sum_ref, other_ref, pos_in, vel_in, pos_ref, vel_ref, stress_ref, line):
    move_tiles(tail_rows, flat_ref, tail_ref, pos_ref, vel_ref, line)
    at = 6 * tail_rows if other_ref.shape == tail_ref.shape else 0
    total = sum_ref[...] + other_ref[at : at + 8, :]
    total = jnp.sum(jnp.sum(total, axis=0, keepdims=True), axis=1, keepdims=True)
    stress_ref[...] = jnp.broadcast_to(total * scale, stress_ref.shape)


def vmem(count):
    return [pl.BlockSpec(memory_space=pltpu.VMEM)] * count


def smem(count):
    return [pl.BlockSpec(memory_space=pltpu.SMEM)] * count


def f32(*shape):
    return jax.ShapeDtypeStruct(shape, jnp.float32)


def per_device(bead_pos, bead_vel, noise_angle, occupancy, image_shift, strain):
    grads = lax.axis_size("grad")
    flows = lax.axis_size("flow")
    tiles = occupancy.shape[1]
    lanes = 2 * tiles
    rows = tiles * TB // (2 * TB)

    def from_mate(x):
        return lax.ppermute(x, "grad", [(g, g ^ 1) for g in range(grads)])

    def from_flow(x, ahead):
        return lax.ppermute(x, "flow", [((f + ahead) % flows, f) for f in range(flows)])

    tail_rows = (grads // 2 + 1) // 2

    turn = pltpu.VMEM((lanes, 2 * TB), jnp.float32)
    prepare = pl.pallas_call(
        prepare_kernel,
        out_shape=(
            f32(6, HALF, lanes), f32(2, HALF, lanes), f32(HALF, lanes),
            f32(FIELDS * HALF + 8, lanes),
        ),
        in_specs=smem(1) + vmem(4),
        out_specs=vmem(4),
        scratch_shapes=[turn, pltpu.VMEM((8, lanes), jnp.int32)],
        name="prepare",
    )
    state, later, live, sent = prepare(
        strain,
        bead_pos.reshape(3, rows, 2 * TB),
        bead_vel.reshape(3, rows, 2 * TB),
        noise_angle.reshape(2, rows, 2 * TB),
        occupancy,
    )

    pair_flops = 35 * 3 * TB * TB * tiles
    cost = pl.CostEstimate(flops=pair_flops, bytes_accessed=1 << 19, transcendentals=0)
    partners = pltpu.VMEM((FIELDS, 3 * TB, lanes), jnp.float32)
    own = pltpu.VMEM((FIELDS, HALF, lanes), jnp.float32)
    cyclic = [pltpu.VMEM((FIELDS, 3 * HALF, lanes), jnp.float32)] * 2
    backs = [pltpu.VMEM((3, 3 * HALF, lanes), jnp.float32)] * (2 * BACKS)
    sums = []
    for step in range(2):
        last = step == 1
        mate = from_mate(sent)
        other = lax.ppermute(sent, "grad", [(g, (g + 2 * (g % 2) - 1) % grads) for g in range(grads)])
        mate_force, given, edges = pl.pallas_call(
            functools.partial(mate_kernel, step),
            out_shape=(f32(3, HALF, lanes), f32(3 * HALF + 8, lanes), f32(16, lanes)),
            in_specs=smem(1) + vmem(4),
            out_specs=vmem(3),
            scratch_shapes=[own, *cyclic, *backs],
            cost_estimate=cost,
            name=f"mate_pairs_{step}",
        )(strain, state, sent, live, mate)
        other, given = lax.optimization_barrier((other, given))
        taken = from_mate(given)
        left = from_flow(edges, -1)
        right = left if flows == 2 else from_flow(edges, 1)
        blocks = [other] + [from_flow(other, k) for k in range(1, flows)]
        row_force, row_sum = pl.pallas_call(
            functools.partial(row_kernel, step),
            out_shape=(f32(3, HALF, lanes), f32(8, lanes)),
            in_specs=vmem(3),
            out_specs=vmem(2),
            scratch_shapes=[own, *cyclic, *backs],
            cost_estimate=cost,
            name=f"row_pairs_{step}",
        )(state, sent, live)
        outs = (
            (f32(6, rows, 2 * TB), f32(6 * tail_rows + 8, 2 * TB), f32(8, lanes))
            if last
            else (f32(6, HALF, lanes), f32(FIELDS * HALF + 8, lanes), f32(8, lanes))
        )
        results = pl.pallas_call(
            functools.partial(other_kernel, step, flows, grads),
            out_shape=outs,
            in_specs=smem(2) + vmem(11 + flows + len(sums)),
            out_specs=vmem(len(outs)),
            scratch_shapes=[partners, turn, pltpu.VMEM((4, HALF, lanes), jnp.float32), own],
            cost_estimate=cost,
            name=f"other_pairs_{step}",
        )(strain, image_shift, state, sent, live, later, row_force, row_sum, mate_force, given, taken, left, right, *blocks, *sums)
        if last:
            flat, tail, total = results
        else:
            state, sent, *sums = results

    tail = lax.ppermute(tail, "flow", [(f, (f + 1) % flows) for f in range(flows)])
    if flows & (flows - 1):
        raise NotImplementedError
    partial = tail
    if flows > 2:
        hop = 1
        partial = lax.ppermute(total, "flow", [(f, f ^ hop) for f in range(flows)])
        while 2 * hop < flows:
            hop *= 2
            total = total + partial
            partial = lax.ppermute(total, "flow", [(f, f ^ hop) for f in range(flows)])
    scale = -1.0 / (2.0 * tiles * flows * 2.0 * DEPTH)
    line = pltpu.VMEM((tail_rows + rows + 8, 2 * TB), jnp.float32)
    new_pos, new_vel = pl.pallas_call(
        functools.partial(shift_kernel, tail_rows),
        out_shape=(f32(3, rows, 2 * TB), f32(3, rows, 2 * TB)),
        in_specs=vmem(1),
        out_specs=vmem(2),
        scratch_shapes=[line],
        cost_estimate=cost,
        name="shift",
    )(flat)
    head = min(rows, (tail_rows + 7) // 8 * 8)

    def first(*shape):
        return pl.BlockSpec(shape, lambda i: (0,) * len(shape))

    new_pos, new_vel, stress = pl.pallas_call(
        functools.partial(finish_kernel, scale, tail_rows),
        grid=(1,),
        out_shape=(f32(3, rows, 2 * TB), f32(3, rows, 2 * TB), f32(1, 128)),
        in_specs=[
            first(6, head, 2 * TB), first(*tail.shape), first(*total.shape), first(*partial.shape),
            pl.BlockSpec(memory_space=pl.ANY), pl.BlockSpec(memory_space=pl.ANY),
        ],
        out_specs=(first(3, head, 2 * TB), first(3, head, 2 * TB), first(1, 128)),
        input_output_aliases={4: 0, 5: 1},
        scratch_shapes=[line],
        name="finish",
    )(flat, tail, total, partial, new_pos, new_vel)
    return (
        new_pos.reshape(bead_pos.shape),
        new_vel.reshape(bead_vel.shape),
        stress[0, :1],
    )


def solution(mesh):
    in_specs = (
        P(None, "grad", "flow"),
        P(None, "grad", "flow"),
        P(None, "grad", "flow"),
        P("grad", "flow"),
        P(),
        P(),
    )
    out_specs = (P(None, "grad", "flow"), P(None, "grad", "flow"), P("grad"))
    return jax.shard_map(
        per_device, mesh=mesh, in_specs=in_specs, out_specs=out_specs, check_vma=False
    )
```

```python
import functools
import math

import jax
import jax.numpy as jnp
from jax import lax
from jax.experimental import pallas as pl
from jax.experimental.pallas import tpu as pltpu
from jax.sharding import PartitionSpec as P

TB = 64
HALF = TB // 2

repulsion = 25.0
friction = 4.5
noise_gain = 15.0
time_step = 0.04
shear_rate = 0.25
root_two = 1.4142135623730951

DEPTH = TB / 6.0
UNIT = 1.0 / DEPTH
SPEED = friction * DEPTH**3
KICK = math.sqrt(noise_gain * root_two)
FAR = 1.0e6

FIELDS = 8
TOGETHER = 1
UNROLL = 32
STRIDE = 16
BACKS = 1


def lanes_of(shape):
    return lax.broadcasted_iota(jnp.int32, shape, 1)


def live_beads(occ_ref, occ_tmp, tiles):
    occ_tmp[...] = jnp.zeros_like(occ_tmp)
    occ_tmp[0:1, 0:tiles] = occ_ref[...]
    row = jnp.broadcast_to(occ_tmp[0:1, :], (8, 2 * tiles))
    row = jnp.where(lanes_of(row.shape) < tiles, row, pltpu.roll(row, tiles, 1))
    limit = jnp.broadcast_to(row[0:1, :], (HALF, 2 * tiles))
    upper = (lanes_of(limit.shape) >= tiles).astype(jnp.int32)
    slot = lax.broadcasted_iota(jnp.int32, limit.shape, 0) + HALF * upper
    return (slot < limit).astype(jnp.float32)


def part(ref, field):
    return ref[field * HALF : (field + 1) * HALF, :]


def write_sent(state, kick, live, strain, sent_ref, turn):
    pos_x, pos_y, pos_z, vel_x, vel_y, vel_z = state
    fields = [
        (pos_x + strain * pos_y) * UNIT,
        jnp.where(live > 0.0, pos_y * UNIT, FAR),
        pos_z * UNIT,
        vel_x * SPEED,
        vel_y * SPEED,
        vel_z * SPEED,
        kick[0],
        kick[1],
    ]
    tiles = sent_ref.shape[1] // 2
    for field in range(FIELDS):
        sent_ref[field * HALF : (field + 1) * HALF, :] = fields[field]
    for group in range(2):
        for k in range(4):
            turn[k * HALF : (k + 1) * HALF, :] = fields[4 * group + k]
        turned = turn[...].T
        for side, tile in enumerate((0, tiles - 1)):
            for half in range(2):
                at = FIELDS * HALF + group * 4 + side * 2 + half
                row = half * tiles + tile
                sent_ref[at : at + 1, :] = turned[row : row + 1, :]


def prepare_kernel(strain_ref, pos_ref, vel_ref, noise_ref, occ_ref, state_ref, later_ref, live_ref, sent_ref, turn, occ_tmp):
    tiles = occ_ref.shape[1]
    live = live_beads(occ_ref, occ_tmp, tiles)
    live_ref[...] = live
    rows = pos_ref.shape[1]
    low = lanes_of((rows, 2 * TB)) < TB
    sources = [pos_ref.at[0], pos_ref.at[1], pos_ref.at[2], vel_ref.at[0], vel_ref.at[1], vel_ref.at[2], noise_ref.at[0], noise_ref.at[1]]
    fields = []
    first = lanes_of((HALF, 2 * tiles)) < tiles
    for pair in range(4):
        one = sources[2 * pair][...]
        two = sources[2 * pair + 1][...]
        even = jnp.where(low, one, pltpu.roll(two, TB, 1))
        odd = jnp.where(low, pltpu.roll(one, TB, 1), two)
        for copy in range(2):
            turn[pl.ds(copy * tiles, rows, stride=2), :] = even
            turn[pl.ds(copy * tiles + 1, rows, stride=2), :] = odd
        turned = turn[...].T
        for k in range(2):
            whole = turned[k * TB : (k + 1) * TB]
            fields.append(jnp.where(first, whole[:HALF], whole[HALF:]))
    for k in range(6):
        state_ref[k] = fields[k]
    later_ref[0] = KICK * jnp.cos(fields[7])
    later_ref[1] = KICK * jnp.sin(fields[7])
    kick = (KICK * jnp.cos(fields[6]), KICK * jnp.sin(fields[6]))
    write_sent(fields[:6], kick, live, strain_ref[0], sent_ref, turn)


def place_partners(partners, own_row, outside, offset, shift_x, shift_y, tiles):
    shape = (HALF, 2 * tiles)
    first = lanes_of(shape) < tiles
    widest = jnp.zeros(shape, jnp.float32)
    for field in range(FIELDS):
        here = own_row(field)
        for half in range(2):
            inner = here if half == 0 else pltpu.roll(here, tiles, 1)
            window = jnp.where(first, inner, outside(field, half))
            if offset is not None:
                window = pltpu.roll(window, offset, 1)
            for column in range(3):
                toward = column - 1
                low = window if toward == 0 else pltpu.roll(window, -toward % (2 * tiles), 1)
                high = pltpu.roll(window, tiles - toward, 1)
                placed = jnp.where(first, low, high)
                if field == 0:
                    placed = placed + (2.0 * toward * UNIT + shift_x)
                if field == 1:
                    placed = placed + shift_y
                if field == 2:
                    widest = jnp.maximum(widest, jnp.abs(placed - 0.5))
                at = column * TB + half * HALF
                partners[field, at : at + HALF, :] = placed
    return widest


def interact(me, theirs, one_shift):
    dx = me[0] - theirs[0]
    dy = me[1] - theirs[1]
    dz = me[2] - theirs[2]
    fold = jnp.round(dz)
    if one_shift:
        fold = jnp.clip(fold, -1.0, 1.0)
    dz = dz - fold
    weight = jnp.maximum((UNIT * UNIT - dx * dx) - (dy * dy + dz * dz), 0.0)
    approach = dx * (me[3] - theirs[3]) + dy * (me[4] - theirs[4]) + dz * (me[5] - theirs[5])
    kick = (me[6] * theirs[6] + me[7] * theirs[7]) + repulsion
    size = weight * (kick - weight * approach)
    return size * dx, size * dy, size * dz, dy


def keep_own(own, state_ref, sent_ref, live_ref):
    for field in range(FIELDS):
        own[field] = part(sent_ref, field)
    own[1] = jnp.where(live_ref[...] > 0.0, state_ref[1] * UNIT, -FAR)


def strayed(row_ref):
    return jnp.abs(part(row_ref, 2) - 0.5)


def guarded(widest, run):
    if widest is None:
        run(False)
        return
    near = jnp.max(widest) < 0.74
    pl.when(near)(lambda: run(False))
    pl.when(jnp.logical_not(near))(lambda: run(True))


def one_sided(own, partners, count, one_shift, sums_ref):
    for piece in range(HALF // 8):
        rows = slice(piece * 8, piece * 8 + 8)
        me = [own[field, rows, :] for field in range(FIELDS)]

        def body(step, sums):
            for inner in range(UNROLL):
                at = step * UNROLL + inner
                theirs = [partners[field, pl.ds(at, 8, stride=0), :] for field in range(FIELDS)]
                fx, fy, fz, dy = interact(me, theirs, one_shift)
                sums = (sums[0] + fx, sums[1] + fy, sums[2] + fz, sums[3] + fx * dy)
            return sums

        zero = jnp.zeros((8, own.shape[2]), jnp.float32)
        sums = lax.fori_loop(0, count // UNROLL, body, (zero,) * 4)
        for k in range(4):
            sums_ref[k, rows, :] = sums[k]


def both_sided(own, cyclic, low, count, one_shift, force_ref, backs):
    pieces = HALF // 8
    stride = STRIDE if backs else 1

    def body(step, sums):
        sums = list(sums)
        for inner in range(stride):
            start = low + step * stride + inner
            for piece in range(pieces):
                at = start + piece * 8
                me = [own[field, piece * 8 : piece * 8 + 8, :] for field in range(FIELDS)]
                theirs = [cyclic[field, pl.ds(at, 8), :] for field in range(FIELDS)]
                push = interact(me, theirs, one_shift)
                for k in range(3):
                    sums[piece * 3 + k] = sums[piece * 3 + k] + push[k]
                    if backs:
                        back = backs[inner % BACKS]
                        back[k, pl.ds(at, 8), :] = back[k, pl.ds(at, 8), :] + push[k]
        return tuple(sums)

    spots = [(k, slice(piece * 8, piece * 8 + 8)) for piece in range(pieces) for k in range(3)]
    init = tuple(force_ref[k, rows, :] for k, rows in spots)
    sums = lax.fori_loop(0, count // stride, body, init)
    for (k, rows), value in zip(spots, sums):
        force_ref[k, rows, :] = value


def fill_cyclic(cyclic, row_ref, column, shift_x, shift_y):
    lanes = row_ref.shape[1]
    tiles = lanes // 2
    for field in range(FIELDS):
        value = part(row_ref, field)
        if column:
            value = pltpu.roll(value, lanes - 1, 1)
        if field == 0:
            value = value + (2.0 * column * UNIT + shift_x)
        if field == 1:
            value = value + shift_y
            if column:
                value = jnp.where(lanes_of(value.shape) % tiles == tiles - 1, FAR, value)
        cyclic[field, 0:HALF, :] = value
        cyclic[field, HALF : 2 * HALF, :] = pltpu.roll(value, tiles, 1)
        cyclic[field, 2 * HALF : 3 * HALF, :] = value


def clear(backs):
    for back in backs:
        back[...] = jnp.zeros_like(back)


def fold_back(backs, k, column):
    total = backs[0][k]
    for back in backs[1:]:
        total = total + back[k]
    folded = total[:HALF] + total[2 * HALF :] + pltpu.roll(total[HALF : 2 * HALF], total.shape[1] // 2, 1)
    return pltpu.roll(folded, 1, 1) if column else folded


def edge_rows(own_edge, mate_edge, side):
    lane = lanes_of(own_edge.shape)
    width = own_edge.shape[1]
    rows = []
    for field in range(FIELDS):
        group, k = divmod(field, 4)
        value = None
        for place, (edge, half) in enumerate(((own_edge, 0), (own_edge, 1), (mate_edge, 0), (mate_edge, 1))):
            at = group * 4 + side * 2 + half
            turned = pltpu.roll(edge, (place - k) * HALF % width, 1)
            row = jnp.broadcast_to(turned[at : at + 1, :], edge.shape)
            value = row if value is None else jnp.where(lane >= place * HALF, row, value)
        rows.append(value)
    return rows


def edge_pairs(own, left_ref, right_ref, side, strain, one_shift, found):
    lanes = own.shape[2]
    tiles = lanes // 2
    lane = lanes_of((8, lanes))
    for tile, ref, at, column in ((0, left_ref, 1, -1.0), (tiles - 1, right_ref, 0, 1.0)):
        theirs = edge_rows(ref[0:8, :], ref[8:16, :], at)
        of_mate = (lanes_of(theirs[0].shape) >= 2 * HALF).astype(jnp.float32)
        theirs[0] = theirs[0] + (2.0 * column * UNIT + side * strain * UNIT * of_mate)
        theirs[1] = theirs[1] + side * UNIT * of_mate
        for half in range(2):
            spot = half * tiles + tile
            for piece in range(HALF // 8):
                rows = slice(piece * 8, piece * 8 + 8)
                me = [
                    jnp.broadcast_to(own[field, rows, :][:, spot : spot + 1], (8, lanes))
                    for field in range(FIELDS)
                ]
                fx, fy, fz, dy = interact(me, theirs, one_shift)
                for k, value in enumerate((fx, fy, fz, fx * dy)):
                    total = jnp.sum(value, axis=1, keepdims=True)
                    found[k, rows, :] = found[k, rows, :] + jnp.where(lane == spot, total, 0.0)


def side_of(other):
    even = 1 - lax.axis_index("grad") % 2
    return (1 - 2 * even if other else 2 * even - 1).astype(jnp.float32)


def row_kernel(step, state_ref, sent_ref, live_ref, force_ref, sum_ref, own, same, follow, *backs):
    keep_own(own, state_ref, sent_ref, live_ref)
    fill_cyclic(same, sent_ref, 0, 0.0, 0.0)
    fill_cyclic(follow, sent_ref, 1, 0.0, 0.0)
    clear(backs)
    force_ref[...] = jnp.zeros_like(force_ref)
    here, beyond = backs[:BACKS], backs[BACKS:]

    def run(one_shift):
        both_sided(own, same, 0, HALF, one_shift, force_ref, here)
        both_sided(own, same, HALF, 1, one_shift, force_ref, ())
        both_sided(own, follow, 0, TB, one_shift, force_ref, beyond)

    guarded(strayed(sent_ref) if step else None, run)
    for k in range(3):
        force_ref[k] = force_ref[k] - (fold_back(here, k, 0) + fold_back(beyond, k, 1))
    total = jnp.zeros(sum_ref.shape, jnp.float32)
    for piece in range(HALF // 8):
        rows = slice(piece * 8, piece * 8 + 8)
        kinetic = state_ref[3, rows, :] * state_ref[4, rows, :]
        virial = DEPTH**3 * force_ref[0, rows, :] * state_ref[1, rows, :]
        total = total + live_ref[rows, :] * (kinetic + virial)
    sum_ref[...] = total


def mate_kernel(step, strain_ref, state_ref, sent_ref, live_ref, mate_ref, force_ref, given_ref, edge_ref, own, same, follow, *backs):
    strain = strain_ref[0] + step * shear_rate * time_step
    side = side_of(False)
    keep_own(own, state_ref, sent_ref, live_ref)
    fill_cyclic(same, mate_ref, 0, side * strain * UNIT, side * UNIT)
    fill_cyclic(follow, mate_ref, 1, side * strain * UNIT, side * UNIT)
    clear(backs)
    force_ref[...] = jnp.zeros_like(force_ref)
    here, beyond = backs[:BACKS], backs[BACKS:]
    low = lax.axis_index("grad") % 2

    def run(one_shift):
        both_sided(own, same, low, HALF, one_shift, force_ref, here)
        both_sided(own, follow, 0, TB, one_shift, force_ref, beyond)

    guarded(jnp.maximum(strayed(sent_ref), strayed(mate_ref)) if step else None, run)
    given = [fold_back(here, k, 0) + fold_back(beyond, k, 1) for k in range(3)]
    for k in range(3):
        given_ref[k * HALF : (k + 1) * HALF, :] = given[k]
    virial = own[1] * force_ref[0] - (part(mate_ref, 1) + side * UNIT) * given[0]
    given_ref[3 * HALF : 3 * HALF + 8, :] = sum(virial[at : at + 8] for at in range(0, HALF, 8))
    edge_ref[0:8, :] = sent_ref[FIELDS * HALF : FIELDS * HALF + 8, :]
    edge_ref[8:16, :] = mate_ref[FIELDS * HALF : FIELDS * HALF + 8, :]


def other_kernel(step, flows, grads, strain_ref, shift_ref, *refs):
    refs = list(refs)
    state_ref, sent_ref, live_ref, later_ref, row_force, row_sum, mate_force, given, taken, left, right = refs[:11]
    blocks = refs[11 : 11 + flows]
    rest = refs[11 + flows :]
    last = step == 1
    if last:
        old_sum, rest = rest[0], rest[1:]
    strain = strain_ref[0] + step * shear_rate * time_step
    tiles = sent_ref.shape[1] // 2
    lanes = 2 * tiles
    partners, turn, found, own = rest[-4:]
    grad = lax.axis_index("grad")
    side = side_of(True)
    whole = tiles * flows
    shift = lax.rem(shift_ref[0], whole)
    start = jnp.where(grad == 0, shift, jnp.where(grad == grads - 1, lax.rem(whole - shift, whole), 0))
    block = start // tiles
    offset = lax.rem(lanes - lax.rem(start, tiles), lanes)

    def pick(field, ahead):
        value = part(blocks[0], field)
        for k in range(1, flows):
            value = jnp.where(lax.rem(block + ahead, flows) == k, part(blocks[k], field), value)
        return value

    def outside(field, half):
        beyond = pick(field, 1)
        if flows > 2:
            lane = lanes_of(beyond.shape)
            final = jnp.logical_and(lane % tiles == tiles - 1, offset == 0)
            beyond = jnp.where(final, pick(field, flows - 1), beyond)
        return pltpu.roll(beyond, tiles, 1) if half == 0 else beyond

    widest = place_partners(
        partners, lambda field: pick(field, 0), outside, offset, side * strain * UNIT, side * UNIT, tiles
    )
    keep_own(own, state_ref, sent_ref, live_ref)
    widest = jnp.maximum(widest, strayed(sent_ref))
    for ref in (left, right):
        lane = lanes_of(ref.shape)
        row = lax.broadcasted_iota(jnp.int32, ref.shape, 0)
        is_z = jnp.logical_and(row % 8 < 4, lane // HALF == 2)
        reach = jnp.where(is_z, jnp.abs(ref[...] - 0.5), 0.0)
        widest = jnp.maximum(widest, jnp.concatenate([reach, reach], 0))

    def run(one_shift):
        one_sided(own, partners, 3 * TB, one_shift, found)
        edge_pairs(own, left, right, side_of(False), strain, one_shift, found)

    guarded(widest if step else None, run)
    total = row_sum[...] + (0.5 * DEPTH**4) * (given[3 * HALF : 3 * HALF + 8, :] + taken[3 * HALF : 3 * HALF + 8, :])
    if last:
        total = total + old_sum[...]
    force = []
    for k in range(3):
        value = found[k] + (row_force[k] + (mate_force[k] - part(taken, k)))
        force.append(value * (live_ref[...] * DEPTH**3))
    for piece in range(HALF // 8):
        rows = slice(piece * 8, piece * 8 + 8)
        total = total + live_ref[rows, :] * (0.5 * DEPTH**4 * found[3, rows, :])
    state = [state_ref[k] for k in range(6)]
    vel_x = state[3] + time_step * (force[0] - shear_rate * state[4])
    vel_y = state[4] + time_step * force[1]
    vel_z = state[5] + time_step * force[2]
    pos_x = state[0] + time_step * (vel_x - strain * vel_y)
    pos_y = state[1] + time_step * vel_y
    pos_z = state[2] + time_step * vel_z
    state = [pos_x, pos_y, pos_z, vel_x, vel_y, vel_z]
    if not last:
        new_state, new_sent, new_sum = rest[:3]
        for k in range(6):
            new_state[k] = state[k]
        new_sum[...] = total
        later = strain + shear_rate * time_step
        write_sent(state, (later_ref[0], later_ref[1]), live_ref[...], later, new_sent, turn)
        return
    flat_ref, tail_ref, new_sum = rest[:3]
    tail_rows = (grads // 2 + 1) // 2
    parity = lax.rem(grad, 2).astype(jnp.float32)
    state[0] = pos_x + parity + pos_y
    new_sum[...] = total
    rows = tiles // 2
    lane = lanes_of((rows, 2 * TB))
    for group in range(2):
        for k in range(4):
            if 4 * group + k < 6:
                turn[k * HALF : (k + 1) * HALF, :] = state[4 * group + k]
        turn[...] = turn[...].T
        for k in range(4):
            if 4 * group + k >= 6:
                continue
            value = None
            for odd in range(2):
                for half in range(2):
                    piece = turn[pl.ds(half * tiles + odd, rows, stride=2), :]
                    target = odd * TB + half * HALF
                    piece = pltpu.roll(piece, (target - k * HALF) % (2 * TB), 1)
                    value = piece if value is None else jnp.where(lane >= target, piece, value)
            flat_ref[4 * group + k] = value
            at = (4 * group + k) * tail_rows
            tail_ref[at : at + tail_rows, :] = value[rows - tail_rows :, :]
    tail_ref[6 * tail_rows : 6 * tail_rows + 8, :] = total


def shift_kernel(tail_rows, flat_ref, pos_ref, vel_ref, line):
    move_tiles(tail_rows, flat_ref, None, pos_ref, vel_ref, line)


def move_tiles(tail_rows, flat_ref, tail_ref, pos_ref, vel_ref, line):
    rows = flat_ref.shape[1]
    skip = 2 * tail_rows - lax.axis_index("grad") // 2
    lane = lanes_of((rows, 2 * TB))
    row0 = skip // 2
    odd = lax.rem(skip, 2)
    for k in range(6):
        if tail_ref is None:
            line[0:tail_rows, :] = jnp.zeros((tail_rows, 2 * TB), jnp.float32)
        else:
            line[0:tail_rows, :] = tail_ref[k * tail_rows : (k + 1) * tail_rows, :]
        line[tail_rows : tail_rows + rows, :] = flat_ref[k]
        one = line[pl.ds(row0, rows), :]
        two = line[pl.ds(row0 + odd, rows), :]
        swapped = jnp.where(lane < TB, pltpu.roll(one, TB, 1), pltpu.roll(two, TB, 1))
        value = jnp.where(odd > 0, swapped, one)
        if k < 3:
            pos_ref[k] = value
        else:
            vel_ref[k - 3] = value


def finish_kernel(scale, tail_rows, flat_ref, tail_ref, sum_ref, other_ref, pos_in, vel_in, pos_ref, vel_ref, stress_ref, line):
    move_tiles(tail_rows, flat_ref, tail_ref, pos_ref, vel_ref, line)
    at = 6 * tail_rows if other_ref.shape == tail_ref.shape else 0
    total = sum_ref[...] + other_ref[at : at + 8, :]
    total = jnp.sum(jnp.sum(total, axis=0, keepdims=True), axis=1, keepdims=True)
    stress_ref[...] = jnp.broadcast_to(total * scale, stress_ref.shape)


def vmem(count):
    return [pl.BlockSpec(memory_space=pltpu.VMEM)] * count


def smem(count):
    return [pl.BlockSpec(memory_space=pltpu.SMEM)] * count


def f32(*shape):
    return jax.ShapeDtypeStruct(shape, jnp.float32)


def per_device(bead_pos, bead_vel, noise_angle, occupancy, image_shift, strain):
    grads = lax.axis_size("grad")
    flows = lax.axis_size("flow")
    tiles = occupancy.shape[1]
    lanes = 2 * tiles
    rows = tiles * TB // (2 * TB)

    def from_mate(x):
        return lax.ppermute(x, "grad", [(g, g ^ 1) for g in range(grads)])

    def from_flow(x, ahead):
        return lax.ppermute(x, "flow", [((f + ahead) % flows, f) for f in range(flows)])

    tail_rows = (grads // 2 + 1) // 2

    turn = pltpu.VMEM((lanes, 2 * TB), jnp.float32)
    prepare = pl.pallas_call(
        prepare_kernel,
        out_shape=(
            f32(6, HALF, lanes), f32(2, HALF, lanes), f32(HALF, lanes),
            f32(FIELDS * HALF + 8, lanes),
        ),
        in_specs=smem(1) + vmem(4),
        out_specs=vmem(4),
        scratch_shapes=[turn, pltpu.VMEM((8, lanes), jnp.int32)],
        name="prepare",
    )
    state, later, live, sent = prepare(
        strain,
        bead_pos.reshape(3, rows, 2 * TB),
        bead_vel.reshape(3, rows, 2 * TB),
        noise_angle.reshape(2, rows, 2 * TB),
        occupancy,
    )

    pair_flops = 35 * 3 * TB * TB * tiles
    cost = pl.CostEstimate(flops=pair_flops, bytes_accessed=1 << 19, transcendentals=0)
    partners = pltpu.VMEM((FIELDS, 3 * TB, lanes), jnp.float32)
    own = pltpu.VMEM((FIELDS, HALF, lanes), jnp.float32)
    cyclic = [pltpu.VMEM((FIELDS, 3 * HALF, lanes), jnp.float32)] * 2
    backs = [pltpu.VMEM((3, 3 * HALF, lanes), jnp.float32)] * (2 * BACKS)
    sums = []
    for step in range(2):
        last = step == 1
        mate = from_mate(sent)
        other = lax.ppermute(sent, "grad", [(g, (g + 2 * (g % 2) - 1) % grads) for g in range(grads)])
        mate_force, given, edges = pl.pallas_call(
            functools.partial(mate_kernel, step),
            out_shape=(f32(3, HALF, lanes), f32(3 * HALF + 8, lanes), f32(16, lanes)),
            in_specs=smem(1) + vmem(4),
            out_specs=vmem(3),
            scratch_shapes=[own, *cyclic, *backs],
            cost_estimate=cost,
            name=f"mate_pairs_{step}",
        )(strain, state, sent, live, mate)
        other, given = lax.optimization_barrier((other, given))
        taken = from_mate(given)
        left = from_flow(edges, -1)
        right = left if flows == 2 else from_flow(edges, 1)
        blocks = [other] + [from_flow(other, k) for k in range(1, flows)]
        row_force, row_sum = pl.pallas_call(
            functools.partial(row_kernel, step),
            out_shape=(f32(3, HALF, lanes), f32(8, lanes)),
            in_specs=vmem(3),
            out_specs=vmem(2),
            scratch_shapes=[own, *cyclic, *backs],
            cost_estimate=cost,
            name=f"row_pairs_{step}",
        )(state, sent, live)
        outs = (
            (f32(6, rows, 2 * TB), f32(6 * tail_rows + 8, 2 * TB), f32(8, lanes))
            if last
            else (f32(6, HALF, lanes), f32(FIELDS * HALF + 8, lanes), f32(8, lanes))
        )
        results = pl.pallas_call(
            functools.partial(other_kernel, step, flows, grads),
            out_shape=outs,
            in_specs=smem(2) + vmem(11 + flows + len(sums)),
            out_specs=vmem(len(outs)),
            scratch_shapes=[partners, turn, pltpu.VMEM((4, HALF, lanes), jnp.float32), own],
            cost_estimate=cost,
            name=f"other_pairs_{step}",
        )(strain, image_shift, state, sent, live, later, row_force, row_sum, mate_force, given, taken, left, right, *blocks, *sums)
        if last:
            flat, tail, total = results
        else:
            state, sent, *sums = results

    tail = lax.ppermute(tail, "flow", [(f, (f + 1) % flows) for f in range(flows)])
    if flows & (flows - 1):
        raise NotImplementedError
    partial = tail
    if flows > 2:
        hop = 1
        partial = lax.ppermute(total, "flow", [(f, f ^ hop) for f in range(flows)])
        while 2 * hop < flows:
            hop *= 2
            total = total + partial
            partial = lax.ppermute(total, "flow", [(f, f ^ hop) for f in range(flows)])
    scale = -1.0 / (2.0 * tiles * flows * 2.0 * DEPTH)
    line = pltpu.VMEM((tail_rows + rows + 8, 2 * TB), jnp.float32)
    new_pos, new_vel = pl.pallas_call(
        functools.partial(shift_kernel, tail_rows),
        out_shape=(f32(3, rows, 2 * TB), f32(3, rows, 2 * TB)),
        in_specs=vmem(1),
        out_specs=vmem(2),
        scratch_shapes=[line],
        cost_estimate=cost,
        name="shift",
    )(flat)
    head = min(rows, (tail_rows + 7) // 8 * 8)

    def first(*shape):
        return pl.BlockSpec(shape, lambda i: (0,) * len(shape))

    new_pos, new_vel, stress = pl.pallas_call(
        functools.partial(finish_kernel, scale, tail_rows),
        grid=(1,),
        out_shape=(f32(3, rows, 2 * TB), f32(3, rows, 2 * TB), f32(1, 128)),
        in_specs=[
            first(6, head, 2 * TB), first(*tail.shape), first(*total.shape), first(*partial.shape),
            pl.BlockSpec(memory_space=pl.ANY), pl.BlockSpec(memory_space=pl.ANY),
        ],
        out_specs=(first(3, head, 2 * TB), first(3, head, 2 * TB), first(1, 128)),
        input_output_aliases={4: 0, 5: 1},
        scratch_shapes=[line],
        name="finish",
    )(flat, tail, total, partial, new_pos, new_vel)
    return (
        new_pos.reshape(bead_pos.shape),
        new_vel.reshape(bead_vel.shape),
        stress[0, :1],
    )


def solution(mesh):
    in_specs = (
        P(None, "grad", "flow"),
        P(None, "grad", "flow"),
        P(None, "grad", "flow"),
        P("grad", "flow"),
        P(),
        P(),
    )
    out_specs = (P(None, "grad", "flow"), P(None, "grad", "flow"), P("grad"))
    return jax.shard_map(
        per_device, mesh=mesh, in_specs=in_specs, out_specs=out_specs, check_vma=False
    )
```
